128 devices in a mesh: grp: 16 (over z, y), tok: 8 (over x, core).
Axes of the slice: x: 4, y: 4, z: 4, core: 2. Of those that a mesh axis runs over, the one named last changes fastest.
Arguments:
- queries: bfloat16 [16384, 5120], P(('grp', 'tok')), may hold values from -6 to 6
- rotated_keys_values: bfloat16 [16384, 2048], P(('grp', 'tok')), may hold values from -6 to 6
- prompt_window_index: int32 [16, 1024], P('grp', 'tok'), may hold values from 0 to 1, never falling along the last dimension, each value on 1 to 768 neighbouring positions
- residual: bfloat16 [16384, 5120], P(('grp', 'tok')), may hold values from -8 to 8
- ffn_gain: float32 [5120], replicated, may hold values from 0.1 to 1.9
- gate_weight: bfloat16 [5120, 8192], P(None, 'grp'), may hold values from -0.078125 to 0.078125
- up_weight: bfloat16 [5120, 8192], P(None, 'grp'), may hold values from -0.078125 to 0.078125
- paged_cache: bfloat16 [2048, 16, 2048], P(('grp', 'tok')), may hold values from -6 to 6
- page_table: int32 [16, 128], P('grp'), may hold values from 0 to 127, each once within a row
Outputs:
- attended: bfloat16 [16384, 5120], P(('grp', 'tok'))
- hidden: bfloat16 [16384, 8192], P(('grp', 'tok'))
- cache_out: bfloat16 [2048, 16, 2048], P(('grp', 'tok'))
The draws below stay inside these ranges and needn't reach their ends.
All inputs are finite; a program needn't handle non-finite values.
Results may differ from the reference program's by a relative error of at most 0.012.
Values may be sent and summed in bfloat16 or wider, within the bound.
A program may use at most 128 MiB of HBM per device.

```python
import math
import jax
import jax.numpy as jnp
import numpy as np
from jax import lax

MODEL_WIDTH = 5120
QUERY_HEADS = 40
KEY_VALUE_HEADS = 8
HEAD_SIZE = 128
GATED_UNITS = 8192
TOK_DEV = 128
PAGE_TOKENS = 16
PROMPTS = 2
GT = 1024
TOTAL_TOKENS = 16384
MOST = 768
GROUP_SLOTS = 128
N_GRP = 16
N_TOK = 8


def draw_queries(key, part):
    unrotated = jnp.clip(jax.random.normal(jax.random.fold_in(key, 1), (TOTAL_TOKENS, QUERY_HEADS * HEAD_SIZE), jnp.float32), -6.0, 6.0)
    return unrotated.astype(jnp.bfloat16)


def draw_rotated_keys_values(key, part):
    unrotated = jnp.clip(jax.random.normal(jax.random.fold_in(key, 2), (TOTAL_TOKENS, 2 * KEY_VALUE_HEADS * HEAD_SIZE), jnp.float32), -6.0, 6.0)
    return unrotated.astype(jnp.bfloat16)


def draw_residual(key, part):
    noise = jnp.clip(jax.random.normal(jax.random.fold_in(key, 3), (TOTAL_TOKENS, MODEL_WIDTH), jnp.float32), -6.0, 6.0)
    column_scale = jnp.exp(jax.random.uniform(jax.random.fold_in(key, 4), (MODEL_WIDTH,), jnp.float32, math.log(0.3), math.log(3.0)))
    spread = 0.7
    row_scale = jnp.exp(jax.random.uniform(jax.random.fold_in(key, 5), (TOTAL_TOKENS, 1), jnp.float32, -spread, spread))
    value = 0.25 * noise * column_scale * row_scale
    return jnp.clip(value, -8.0, 8.0).astype(jnp.bfloat16)


def levels(key, dims, cuts, least, top_value):
    factor_of = 1.0
    for dim, parts in cuts:
        heights = jax.random.uniform(jax.random.fold_in(jax.random.fold_in(key, 6), dim), (parts,), jnp.float32, least / len(cuts), top_value / len(cuts))
        factor_of = factor_of * jnp.repeat(jnp.exp(heights), dims[dim] // parts).reshape((-1,) + (1,) * (len(dims) - 1 - dim))
    return factor_of


def length_profile(number_of, total, bound, slope):
    portions = [(1 << 20) // math.isqrt(rank ** slope) + 1 for rank in range(2, number_of + 1)]
    surplus, holding = total - bound - (number_of - 1), [1] * (number_of - 1)
    while surplus > 0:
        movable = [i for i in range(number_of - 1) if holding[i] < bound]
        whole, left = sum([portions[i] for i in movable]), surplus
        for i in movable:
            extra = min(bound - holding[i], max(1, left * portions[i] // whole), surplus)
            holding[i] = holding[i] + extra
            surplus = surplus - extra
    return np.array([bound] + holding)


def uneven(rng, amount, total, most, lean):
    if amount == 2:
        one = jax.random.randint(rng, (), max(1, total - most), min(most, total - 1) + 1)
        return jnp.stack([one, total - one])
    sizes = jnp.asarray(length_profile(amount, total, most, lean), jnp.int32)
    twos = (amount - 1) // 2
    giver, sink = sizes[1:1 + 2 * twos:2], sizes[2:2 + 2 * twos:2]
    slack = jnp.minimum(giver - 1, most - sink)
    moved = jax.random.randint(jax.random.fold_in(rng, 1), (twos,), 0, 1 << 20) % (slack + 1)
    sizes = sizes.at[1:1 + 2 * twos:2].set(giver - moved).at[2:2 + 2 * twos:2].set(sink + moved)
    return sizes[jax.random.permutation(jax.random.fold_in(rng, 2), amount)]


def centred(key, shape, width, reach, cuts=(), held_as=jnp.bfloat16):
    level = levels(key, shape, cuts, -0.22, 0.18) if cuts else 1.0
    entries = jax.random.normal(key, shape, jnp.float32) * width * level
    return jnp.minimum(jnp.maximum(entries, -reach), reach).astype(held_as)


def setup_inputs(seed: int = 0) -> dict:
    keys = jax.random.split(jax.random.key(seed), 10)
    return {
        "queries": draw_queries(jax.random.fold_in(keys[9], 71), 0),
        "rotated_keys_values": draw_rotated_keys_values(jax.random.fold_in(keys[9], 71), 0),
        "prompt_window_index": jax.vmap(lambda own: jnp.searchsorted(jnp.cumsum(uneven(own, PROMPTS, GT, MOST, 2)), jnp.arange(GT), side="right"))(jax.random.split(keys[2], N_GRP)).reshape((N_GRP, GT)).astype(jnp.int32),
        "residual": draw_residual(jax.random.fold_in(keys[9], 71), 0),
        "ffn_gain": jnp.clip(1.0 + 0.18 * jax.random.normal(keys[4], (MODEL_WIDTH,), jnp.float32), 0.1, 1.9),
        "gate_weight": centred(keys[5], (MODEL_WIDTH, GATED_UNITS), MODEL_WIDTH ** -0.5, 0.078125, ((1, 16),)),
        "up_weight": centred(keys[6], (MODEL_WIDTH, GATED_UNITS), MODEL_WIDTH ** -0.5, 0.078125, ((1, 16),)),
        "paged_cache": centred(keys[7], (N_GRP * GROUP_SLOTS, PAGE_TOKENS, 2 * KEY_VALUE_HEADS * HEAD_SIZE), 1.0, 6.0, ((0, 128),)),
        "page_table": jax.vmap(lambda own: jax.random.permutation(own, GROUP_SLOTS))(jax.random.split(keys[8], N_GRP)).reshape((N_GRP, GROUP_SLOTS)).astype(jnp.int32),
    }


MASK_FILLER = -1e+30

def attend_group(group_query, group_key_value, group_seg):
    count_of_rows = group_query.shape[0]
    grouped_rows = group_query.reshape(count_of_rows, KEY_VALUE_HEADS, QUERY_HEADS // KEY_VALUE_HEADS, HEAD_SIZE).astype(jnp.float32)
    rows_of_keys = group_key_value[:, :KEY_VALUE_HEADS * HEAD_SIZE].reshape(count_of_rows, KEY_VALUE_HEADS, HEAD_SIZE).astype(jnp.float32)
    rows_of_values = group_key_value[:, KEY_VALUE_HEADS * HEAD_SIZE:].reshape(count_of_rows, KEY_VALUE_HEADS, HEAD_SIZE).astype(jnp.float32)
    scores = jnp.einsum('qgrd,kgd->qgrk', grouped_rows, rows_of_keys) * (1.0 / math.sqrt(HEAD_SIZE))
    position = jnp.arange(count_of_rows)
    live_mask = (group_seg[:, None] == group_seg[None, :]) & (position[None, :] <= position[:, None])
    live_mask = live_mask[:, None, None, :]
    scores = jnp.where(live_mask, scores, MASK_FILLER)
    row_max = lax.optimization_barrier(jnp.max(scores, axis=-1, keepdims=True))
    weights = jnp.where(live_mask, jnp.exp(scores - row_max), 0.0)
    denominator = lax.optimization_barrier(jnp.sum(weights, axis=-1))
    rounded = lax.optimization_barrier(weights.astype(jnp.bfloat16)).astype(jnp.float32)
    summed = jnp.einsum('qgrk,kgd->qgrd', rounded, rows_of_values) / denominator[..., None]
    return summed.reshape(count_of_rows, QUERY_HEADS * HEAD_SIZE).astype(jnp.bfloat16)

def reference(queries, rotated_keys_values, prompt_window_index, residual, ffn_gain, gate_weight, up_weight, paged_cache, page_table):
    rows_of_group = TOK_DEV * N_TOK

    def single_group(group_items):
        group_query, group_key_value, group_seg, group_res = group_items
        attention = attend_group(group_query, group_key_value, group_seg)
        attended = (group_res.astype(jnp.float32) + attention.astype(jnp.float32)).astype(jnp.bfloat16)
        widened = attended.astype(jnp.float32)
        normed = (widened * lax.rsqrt(lax.optimization_barrier(jnp.mean(widened * widened, axis=-1, keepdims=True)) + 1e-06) * ffn_gain).astype(jnp.bfloat16)
        gate_sum = jnp.dot(normed, gate_weight, preferred_element_type=jnp.float32)
        up_sum = jnp.dot(normed, up_weight, preferred_element_type=jnp.float32)
        hidden = (jax.nn.silu(gate_sum) * up_sum).astype(jnp.bfloat16)
        return (attended, hidden)
    attended, hidden = lax.map(single_group, (queries.reshape(N_GRP, rows_of_group, QUERY_HEADS * HEAD_SIZE), rotated_keys_values.reshape(N_GRP, rows_of_group, 2 * KEY_VALUE_HEADS * HEAD_SIZE), prompt_window_index, residual.reshape(N_GRP, rows_of_group, MODEL_WIDTH)))
    cache_slot_index = paged_cache.reshape(N_GRP, GROUP_SLOTS, PAGE_TOKENS, 2 * KEY_VALUE_HEADS * HEAD_SIZE)
    newly_written_pages = rotated_keys_values.reshape(N_GRP, rows_of_group // PAGE_TOKENS, PAGE_TOKENS, 2 * KEY_VALUE_HEADS * HEAD_SIZE)
    used_pages = rows_of_group // PAGE_TOKENS

    def write_pages(slots_of_group, table_row, pages_of_group):
        return slots_of_group.at[table_row[:used_pages]].set(pages_of_group)
    cache_slot_index = jax.vmap(write_pages)(cache_slot_index, page_table, newly_written_pages)
    return (attended.reshape(TOTAL_TOKENS, MODEL_WIDTH), hidden.reshape(TOTAL_TOKENS, GATED_UNITS), cache_slot_index.reshape(N_GRP * GROUP_SLOTS, PAGE_TOKENS, 2 * KEY_VALUE_HEADS * HEAD_SIZE))
```

```python
import math

import jax
import jax.numpy as jnp
from jax import lax
from jax.experimental import pallas as pl
from jax.experimental.pallas import tpu as pltpu
from jax.sharding import PartitionSpec as P

HEADS = 40
KV_HEADS = 8
HEAD = 128
GROUP = HEADS // KV_HEADS
PAGE = 16
WIDTH = HEADS * HEAD
COLS = 128
SIDE = 4
N_TOK = 8
MASKED = -1e30
MESH = pl.DeviceIdType.MESH


def kernel(
    q_in,
    kv_in,
    seg_in,
    res_in,
    gain_in,
    gate_in,
    up_in,
    cache_in,
    table_in,
    att_out,
    hid_out,
    cache_out,
    qbuf,
    kvbuf,
    segbuf,
    resbuf,
    cachebuf,
    placedbuf,
    attbuf,
    biasbuf,
    normbuf,
    wbuf,
    hidbuf,
    kv_send,
    kv_recv,
    nrm_send,
    nrm_recv,
    w_send,
    w_recv,
    seg_send,
    seg_recv,
    hid_send,
    hid_recv,
    local_sem,
):
    rows = q_in.shape[0]
    half = rows // 2
    keys = N_TOK * rows
    slots_here = cache_in.shape[0]
    units = gate_in.shape[1]
    g = lax.axis_index("grp")
    t = lax.axis_index("tok")
    x, c = t // 2, t % 2
    z, y = g // SIDE, g % SIDE
    first = c == 0
    p = jnp.where(first, z, y)
    q = jnp.where(first, y, z)
    p_step = jnp.where(first, SIDE, 1)
    q_step = jnp.where(first, 1, SIDE)

    def wrap(v):
        return (v + SIDE) % SIDE

    def grp_of(pp, qq):
        return pp * p_step + qq * q_step

    x_next = (g, wrap(x + 1) * 2 + c)
    x_prev = (g, wrap(x - 1) * 2 + c)
    sibling = (g, x * 2 + 1 - c)
    p_next = (grp_of(wrap(p + 1), q), t)
    p_prev = (grp_of(wrap(p - 1), q), t)
    q_next = (grp_of(p, wrap(q + 1)), t)
    q_prev = (grp_of(p, wrap(q - 1)), t)
    plane = (p_next, p_prev, q_next, q_prev)
    P_NEXT, P_PREV, Q_NEXT, Q_PREV = 0, 1, 2, 3

    barrier = pltpu.get_barrier_semaphore()
    for there in plane:
        pl.semaphore_signal(barrier, inc=1, device_id=there, device_id_type=MESH)
    for d in range(1, N_TOK):
        pl.semaphore_signal(
            barrier, inc=1, device_id=(g, (t + d) % N_TOK), device_id_type=MESH
        )
    pl.semaphore_wait(barrier, N_TOK + 3)

    source = (p + q) % 2 == c
    x_col = pl.multiple_of(x * COLS, COLS)
    own_slot = q * 2 + p // 2
    far_slot = q * 2 + 1 - p // 2
    prev_slot = q * 2 + wrap(p - 1) // 2
    next_slot = q * 2 + wrap(p + 1) // 2

    def piece(slot, m):
        return wbuf.at[slot, :, pl.ds(m * COLS, COLS)]

    def own_piece(m):
        return (gate_in, up_in)[m].at[:, pl.ds(x_col, COLS)]

    def w_copy(slot, m, way, src=None):
        return pltpu.make_async_remote_copy(
            src_ref=piece(slot, m) if src is None else src,
            dst_ref=piece(slot, m),
            send_sem=w_send.at[way, slot * 2 + m],
            recv_sem=w_recv.at[slot * 2 + m],
            device_id=plane[way],
            device_id_type=MESH,
        )

    def w_wait(slot, m):
        w_copy(slot, m, 0).wait_recv()

    @pl.when(source)
    def _():
        for m in range(2):
            for way in range(4):
                w_copy(own_slot, m, way, own_piece(m)).start()

    def ring(buf, send, recv):
        def copy(slot, n_send, n_recv, there, part=None, src=None):
            ref = buf.at[slot]
            if part is not None:
                ref = ref.at[pl.ds(part * half, half)]
            return pltpu.make_async_remote_copy(
                src_ref=ref if src is None else src,
                dst_ref=ref,
                send_sem=send.at[n_send],
                recv_sem=recv.at[n_recv],
                device_id=there,
                device_id_type=MESH,
            )

        prev_s = wrap(x - 1) * 2 + c
        next_s = wrap(x + 1) * 2 + c
        far_s = wrap(x + 2) * 2 + c
        other = 1 - 2 * c

        def begin(src=None):
            copy(t, 0, 0, x_next, src=src).start()
            copy(t, 1, 1, x_prev, src=src).start()
            copy(t, 2, 4, sibling, src=src).start()

        def relay_near():
            copy(prev_s, 0, 0, x_next).wait_recv()
            copy(prev_s, 3, 2, x_next, part=0).start()
            copy(prev_s, 4, 5, sibling).start()
            copy(next_s, 1, 1, x_prev).wait_recv()
            copy(next_s, 5, 3, x_prev, part=1).start()
            copy(next_s, 6, 6, sibling).start()

        def relay_far():
            copy(far_s, 3, 2, x_next, part=0).wait_recv()
            copy(far_s, 7, 7, sibling, part=0).start()
            copy(far_s, 5, 3, x_prev, part=1).wait_recv()
            copy(far_s, 8, 8, sibling, part=1).start()

        def sibling_own():
            copy(t + other, 2, 4, sibling).wait_recv()

        def sibling_near():
            copy(prev_s + other, 4, 5, sibling).wait_recv()
            copy(next_s + other, 6, 6, sibling).wait_recv()

        def sibling_far():
            copy(far_s + other, 7, 7, sibling, part=0).wait_recv()
            copy(far_s + other, 8, 8, sibling, part=1).wait_recv()

        def drain():
            copy(t, 0, 0, x_next).wait_send()
            copy(t, 1, 1, x_prev).wait_send()
            copy(t, 2, 4, sibling).wait_send()
            copy(prev_s, 3, 2, x_next, part=0).wait_send()
            copy(prev_s, 4, 5, sibling).wait_send()
            copy(next_s, 5, 3, x_prev, part=1).wait_send()
            copy(next_s, 6, 6, sibling).wait_send()
            copy(far_s, 7, 7, sibling, part=0).wait_send()
            copy(far_s, 8, 8, sibling, part=1).wait_send()

        return (
            begin,
            relay_near,
            relay_far,
            sibling_own,
            sibling_near,
            sibling_far,
            drain,
        )

    kv_ring = ring(kvbuf, kv_send, kv_recv)
    kv_ring[0](kv_in)

    def seg_copy(d):
        return pltpu.make_async_remote_copy(
            src_ref=seg_in,
            dst_ref=segbuf.at[t],
            send_sem=seg_send,
            recv_sem=seg_recv,
            device_id=(g, (t + d) % N_TOK),
            device_id_type=MESH,
        )

    for d in range(1, N_TOK):
        seg_copy(d).start()

    load_kv = pltpu.make_async_copy(kv_in, kvbuf.at[t], local_sem.at[0])
    load_q = pltpu.make_async_copy(q_in, qbuf, local_sem.at[1])
    load_res = pltpu.make_async_copy(res_in, resbuf, local_sem.at[2])
    load_cache = pltpu.make_async_copy(cache_in, cachebuf, local_sem.at[3])
    load_seg = pltpu.make_async_copy(seg_in, segbuf.at[t], local_sem.at[4])
    load_gate = pltpu.make_async_copy(own_piece(0), piece(own_slot, 0), local_sem.at[5])
    load_up = pltpu.make_async_copy(own_piece(1), piece(own_slot, 1), local_sem.at[6])
    load_kv.start()
    load_q.start()
    load_seg.start()
    load_res.start()
    load_cache.start()

    @pl.when(source)
    def _():
        load_gate.start()
        load_up.start()

    load_seg.wait()
    pltpu.make_async_copy(segbuf.at[pl.ds(0, N_TOK - 1)], segbuf.at[pl.ds(0, N_TOK - 1)], seg_recv).wait()
    own_seg = jnp.broadcast_to(seg_in[...], (rows, rows)).T
    row_id = lax.broadcasted_iota(jnp.int32, (rows, rows), 0) + t * rows
    col_id = lax.broadcasted_iota(jnp.int32, (rows, rows), 1)
    for i in range(N_TOK):
        live = (own_seg == segbuf[i]) & (col_id + i * rows <= row_id)
        biasbuf[:, i * rows : (i + 1) * rows] = jnp.where(live, 0.0, MASKED)

    kv_ring[1]()

    @pl.when(jnp.logical_not(source))
    def _():
        w_wait(prev_slot, 0)
        w_copy(prev_slot, 0, P_NEXT).start()
        w_copy(prev_slot, 0, Q_NEXT).start()
        w_copy(prev_slot, 0, Q_PREV).start()
        w_wait(next_slot, 0)
        w_copy(next_slot, 0, Q_NEXT).start()
        w_copy(next_slot, 0, Q_PREV).start()

    kv_ring[2]()
    load_kv.wait()
    load_q.wait()
    load_res.wait()
    kv_ring[3]()
    kv_ring[4]()
    kv_ring[5]()

    scale = 1.0 / math.sqrt(HEAD)

    def attend(h, squares):
        base = pl.multiple_of(h * (GROUP * HEAD), HEAD)
        queries = jnp.concatenate(
            [qbuf[:, pl.ds(base + j * HEAD, HEAD)] for j in range(GROUP)], axis=0
        )
        k_col = pl.multiple_of(h * HEAD, HEAD)
        k = kvbuf[:, :, pl.ds(k_col, HEAD)].reshape(keys, HEAD)
        v = kvbuf[:, :, pl.ds(k_col + KV_HEADS * HEAD, HEAD)].reshape(keys, HEAD)
        scores = lax.dot_general(
            queries, k, (((1,), (1,)), ((), ())), preferred_element_type=jnp.float32
        )
        scores = scores.reshape(GROUP, rows, keys) + biasbuf[...][None]
        top = jnp.max(scores, axis=-1, keepdims=True)
        weights = jnp.exp((scores - top) * scale)
        total = jnp.sum(weights, axis=-1, keepdims=True)
        weights = weights.astype(jnp.bfloat16).reshape(GROUP * rows, keys)
        out = jnp.dot(weights, v, preferred_element_type=jnp.float32)
        out = (out.reshape(GROUP, rows, HEAD) / total).astype(jnp.bfloat16)
        for j in range(GROUP):
            cols = pl.ds(base + j * HEAD, HEAD)
            a = resbuf[:, cols].astype(jnp.float32) + out[j].astype(jnp.float32)
            a = a.astype(jnp.bfloat16)
            attbuf[:, cols] = a
            a = a.astype(jnp.float32)
            squares = squares + a * a
        return squares

    squares = lax.fori_loop(
        0, KV_HEADS // 2, attend, jnp.zeros((rows, HEAD), jnp.float32)
    )

    @pl.when(jnp.logical_not(source))
    def _():
        w_wait(prev_slot, 1)
        w_copy(prev_slot, 1, Q_NEXT).start()
        w_copy(prev_slot, 1, Q_PREV).start()
        w_wait(next_slot, 1)
        w_copy(next_slot, 1, P_PREV).start()
        w_copy(next_slot, 1, Q_NEXT).start()
        w_copy(next_slot, 1, Q_PREV).start()

    @pl.when(source)
    def _():
        load_gate.wait()
        load_up.wait()
        w_wait(far_slot, 0)
        w_copy(far_slot, 0, Q_NEXT).start()
        w_copy(far_slot, 0, Q_PREV).start()

    squares = lax.fori_loop(KV_HEADS // 2, KV_HEADS, attend, squares)
    mean = jnp.sum(squares, axis=-1, keepdims=True) * (1.0 / WIDTH)
    inverse = lax.rsqrt(mean + 1e-6)

    def norm(h, carry):
        cols = pl.ds(pl.multiple_of(h * (GROUP * HEAD), HEAD), GROUP * HEAD)
        a = attbuf[:, cols].astype(jnp.float32) * inverse * gain_in[:, cols]
        normbuf[t, :, cols] = a.astype(jnp.bfloat16)
        return carry

    lax.fori_loop(0, KV_HEADS, norm, 0)

    nrm_ring = ring(normbuf, nrm_send, nrm_recv)
    nrm_ring[0]()
    store_att = pltpu.make_async_copy(attbuf, att_out, local_sem.at[7])
    store_att.start()

    @pl.when(source)
    def _():
        w_wait(far_slot, 1)
        w_copy(far_slot, 1, Q_NEXT).start()
        w_copy(far_slot, 1, Q_PREV).start()

    prev_row = wrap(q - 1) * 2
    next_row = wrap(q + 1) * 2
    lead = p // 2

    load_cache.wait()
    table = jnp.broadcast_to(table_in[...], (8, table_in.shape[1]))
    page_id = lax.broadcasted_iota(jnp.int32, (table_in.shape[1], keys), 0)
    key_id = lax.broadcasted_iota(jnp.int32, (table_in.shape[1], keys), 1)
    spread = (page_id == key_id // PAGE).astype(jnp.float32).astype(jnp.bfloat16)
    slot_of = jnp.dot(
        table.astype(jnp.float32).astype(jnp.bfloat16),
        spread,
        preferred_element_type=jnp.float32,
    )
    key_row = lax.broadcasted_iota(jnp.int32, (8, keys), 1)
    key_row = (key_row % PAGE).astype(jnp.float32)
    shift = (t * slots_here).astype(jnp.float32)
    goal = ((slot_of - shift) * PAGE + key_row)[:1]
    here = lax.broadcasted_iota(jnp.int32, (slots_here * PAGE, keys), 0)
    picked = (here.astype(jnp.float32) == goal).astype(jnp.float32)
    covered = jnp.sum(picked, axis=-1, keepdims=True) > 0.5
    picked = picked.astype(jnp.bfloat16)
    chunk = 512

    def place(i, carry):
        cols = pl.ds(pl.multiple_of(i * chunk, chunk), chunk)
        rows_kv = kvbuf[:, :, cols].reshape(keys, chunk)
        new = jnp.dot(picked, rows_kv, preferred_element_type=jnp.float32)
        old = cachebuf[:, :, cols].reshape(slots_here * PAGE, chunk)
        both = jnp.where(covered, new, old.astype(jnp.float32)).astype(jnp.bfloat16)
        placedbuf[:, :, cols] = both.reshape(slots_here, PAGE, chunk)
        return carry

    lax.fori_loop(0, kv_in.shape[1] // chunk, place, 0)
    store_cache = pltpu.make_async_copy(placedbuf, cache_out, local_sem.at[8])
    store_cache.start()

    def forward_gate(slot):
        w_wait(slot, 0)
        w_copy(slot, 0, Q_NEXT).start()

    def forward_up(slot):
        w_wait(slot, 1)
        w_copy(slot, 1, Q_PREV).start()

    forward_gate(prev_row + lead)
    forward_gate(prev_row + 1 - lead)
    forward_up(next_row + lead)
    nrm_ring[1]()
    forward_up(next_row + 1 - lead)
    nrm_ring[2]()
    nrm_ring[3]()
    nrm_ring[4]()
    nrm_ring[5]()

    parts = 2
    per = N_TOK // parts

    def project(slot):
        qq = slot // 2
        pp = (slot % 2) * 2 + (c + qq) % 2
        column = pl.multiple_of(grp_of(pp, qq) * units + x_col, COLS)

        def tile(i, carry):
            tokens = normbuf[pl.ds(i * per, per)].reshape(per * rows, WIDTH)
            sums = jnp.dot(tokens, wbuf[slot], preferred_element_type=jnp.float32)
            gate, up = sums[:, :COLS], sums[:, COLS:]
            value = gate / (1.0 + jnp.exp(-gate)) * up
            hidbuf[slot, pl.ds(i * per, per)] = value.astype(jnp.bfloat16).reshape(
                per, rows, COLS
            )
            return carry

        lax.fori_loop(0, parts, tile, 0)
        keep = pltpu.make_async_copy(
            hidbuf.at[slot, t], hid_out.at[:, pl.ds(column, COLS)], local_sem.at[9]
        )
        keep.start()

        def send(d, carry):
            there = (t + d) % N_TOK
            pltpu.make_async_remote_copy(
                src_ref=hidbuf.at[slot, there],
                dst_ref=hid_out.at[:, pl.ds(column, COLS)],
                send_sem=hid_send,
                recv_sem=hid_recv,
                device_id=(g, there),
                device_id_type=MESH,
            ).start()
            return carry

        lax.fori_loop(1, N_TOK, send, 0)
        keep.wait()

    def own_row(i, carry):
        project(q * 2 + i)
        return carry

    lax.fori_loop(0, 2, own_row, 0)

    def near_rows(i, carry):
        slot = jnp.where(i % 2 == 0, prev_row, next_row) + jnp.where(
            i < 2, lead, 1 - lead
        )
        prev = i % 2 == 0

        @pl.when(prev)
        def _():
            w_wait(slot, 1)

        @pl.when(jnp.logical_not(prev))
        def _():
            w_wait(slot, 0)

        project(slot)
        return carry

    lax.fori_loop(0, 4, near_rows, 0)
    far_row = wrap(q + 2) * 2

    def far_rows(i, carry):
        slot = far_row + jnp.where(i == 0, lead, 1 - lead)
        w_wait(slot, 0)
        w_wait(slot, 1)
        project(slot)
        return carry

    lax.fori_loop(0, 2, far_rows, 0)

    store_att.wait()
    store_cache.wait()
    for d in range(1, N_TOK):
        pass
    pltpu.make_async_copy(
        segbuf.at[pl.ds(0, N_TOK - 1)], segbuf.at[pl.ds(0, N_TOK - 1)], seg_send
    ).wait()
    kv_ring[6]()
    nrm_ring[6]()

    @pl.when(source)
    def _():
        for m in range(2):
            for way in range(4):
                w_copy(own_slot, m, way).wait_send()
            w_copy(far_slot, m, Q_NEXT).wait_send()
            w_copy(far_slot, m, Q_PREV).wait_send()

    @pl.when(jnp.logical_not(source))
    def _():
        w_copy(prev_slot, 0, P_NEXT).wait_send()
        w_copy(next_slot, 1, P_PREV).wait_send()
        for m in range(2):
            for slot in (prev_slot, next_slot):
                w_copy(slot, m, Q_NEXT).wait_send()
                w_copy(slot, m, Q_PREV).wait_send()

    for i in range(2):
        w_copy(prev_row + i, 0, Q_NEXT).wait_send()
        w_copy(next_row + i, 1, Q_PREV).wait_send()

    whole = hidbuf.at[:, pl.ds(0, N_TOK - 1)]
    pltpu.make_async_copy(whole, whole, hid_send).wait()
    pltpu.make_async_copy(whole, whole, hid_recv).wait()


def on_device(
    queries,
    rotated_keys_values,
    prompt_window_index,
    residual,
    ffn_gain,
    gate_weight,
    up_weight,
    paged_cache,
    page_table,
):
    rows = queries.shape[0]
    kv_width = rotated_keys_values.shape[1]
    hidden_width = gate_weight.shape[1] * SIDE * SIDE
    any_space = pl.BlockSpec(memory_space=pl.ANY)
    vmem = pl.BlockSpec(memory_space=pltpu.VMEM)
    bf16 = jnp.bfloat16
    dma = pltpu.SemaphoreType.DMA
    outs = pl.pallas_call(
        kernel,
        out_shape=(
            jax.ShapeDtypeStruct(residual.shape, bf16),
            jax.ShapeDtypeStruct((rows, hidden_width), bf16),
            jax.ShapeDtypeStruct(paged_cache.shape, bf16),
        ),
        in_specs=[
            any_space,
            any_space,
            vmem,
            any_space,
            vmem,
            any_space,
            any_space,
            any_space,
            vmem,
        ],
        out_specs=(any_space, any_space, any_space),
        scratch_shapes=[
            pltpu.VMEM(queries.shape, bf16),
            pltpu.VMEM((N_TOK, rows, kv_width), bf16),
            pltpu.VMEM((N_TOK, 1, rows), jnp.int32),
            pltpu.VMEM(residual.shape, bf16),
            pltpu.VMEM(paged_cache.shape, bf16),
            pltpu.VMEM(paged_cache.shape, bf16),
            pltpu.VMEM(residual.shape, bf16),
            pltpu.VMEM((rows, N_TOK * rows), jnp.float32),
            pltpu.VMEM((N_TOK, rows, WIDTH), bf16),
            pltpu.VMEM((8, WIDTH, 2 * COLS), bf16),
            pltpu.VMEM((8, N_TOK, rows, COLS), bf16),
            dma((9,)),
            dma((9,)),
            dma((9,)),
            dma((9,)),
            dma((4, 16)),
            dma((16,)),
            dma(()),
            dma(()),
            dma(()),
            dma(()),
            dma((10,)),
        ],
        compiler_params=pltpu.CompilerParams(
            collective_id=0,
            has_side_effects=True,
            vmem_limit_bytes=63 * 1024 * 1024,
        ),
        name="layer",
    )(
        queries,
        rotated_keys_values,
        prompt_window_index,
        residual,
        ffn_gain.reshape(1, -1),
        gate_weight,
        up_weight,
        paged_cache,
        page_table,
    )
    return tuple(outs)


def solution(mesh):
    in_specs = (
        P(("grp", "tok"), None),
        P(("grp", "tok"), None),
        P("grp", "tok"),
        P(("grp", "tok"), None),
        P(),
        P(None, "grp"),
        P(None, "grp"),
        P(("grp", "tok"), None, None),
        P("grp", None),
    )
    out_specs = (P(("grp", "tok"), None), P(("grp", "tok"), None), P(("grp", "tok"), None, None))
    return jax.shard_map(
        on_device, mesh=mesh, in_specs=in_specs, out_specs=out_specs, check_vma=False
    )
```

```python
import math

import jax
import jax.numpy as jnp
from jax import lax
from jax.experimental import pallas as pl
from jax.experimental.pallas import tpu as pltpu
from jax.sharding import PartitionSpec as P

HEADS = 40
KV_HEADS = 8
HEAD = 128
GROUP = HEADS // KV_HEADS
PAGE = 16
WIDTH = HEADS * HEAD
COLS = 128
SIDE = 4
N_TOK = 8
MASKED = -1e30
MESH = pl.DeviceIdType.MESH


def kernel(
    q_in,
    kv_in,
    seg_in,
    res_in,
    gain_in,
    gate_in,
    up_in,
    cache_in,
    table_in,
    att_out,
    hid_out,
    cache_out,
    qbuf,
    kvbuf,
    segbuf,
    resbuf,
    cachebuf,
    placedbuf,
    attbuf,
    biasbuf,
    statbuf,
    scalebuf,
    normbuf,
    wbuf,
    hidbuf,
    kv_send,
    kv_recv,
    nrm_send,
    nrm_recv,
    w_send,
    w_recv,
    seg_send,
    seg_recv,
    stat_send,
    stat_recv,
    hid_send,
    hid_recv,
    local_sem,
):
    rows = q_in.shape[0]
    half = rows // 2
    keys = N_TOK * rows
    slots_here = cache_in.shape[0]
    units = gate_in.shape[1]
    g = lax.axis_index("grp")
    t = lax.axis_index("tok")
    x, c = t // 2, t % 2
    z, y = g // SIDE, g % SIDE
    def wrap(v):
        return (v + SIDE) % SIDE

    def grp_of(zz, yy):
        return zz * SIDE + yy

    x_next = (g, wrap(x + 1) * 2 + c)
    x_prev = (g, wrap(x - 1) * 2 + c)
    sibling = (g, x * 2 + 1 - c)
    plane = (
        grp_of(wrap(z + 1), y),
        grp_of(wrap(z - 1), y),
        grp_of(z, wrap(y + 1)),
        grp_of(z, wrap(y - 1)),
    )
    P_NEXT, P_PREV, Q_NEXT, Q_PREV = 0, 1, 2, 3

    source = (z + y) % 2 == c
    relay = jnp.logical_not(source)
    x_col = pl.multiple_of(x * COLS, COLS)
    deep = WIDTH // 2

    class Walk:
        def __init__(self, m):
            self.m = m
            self.z_first = c == m
            self.p = jnp.where(self.z_first, z, y)
            self.q = jnp.where(self.z_first, y, z)
            z_ways, y_ways = plane[:2], plane[2:]
            self.ways = [
                (jnp.where(self.z_first, a, b), t)
                for a, b in zip(z_ways + y_ways, y_ways + z_ways)
            ]

        def slot(self, dp, dq):
            pp, qq = wrap(self.p + dp), wrap(self.q + dq)
            zz = jnp.where(self.z_first, pp, qq)
            yy = jnp.where(self.z_first, qq, pp)
            return yy * 2 + zz // 2

        def own(self, h):
            ref = (gate_in, up_in)[self.m]
            return ref.at[pl.ds(h * deep, deep), pl.ds(x_col, COLS)]

        def piece(self, slot, h):
            return wbuf.at[slot, self.m, pl.ds(h * deep, deep)]

        def copy(self, slot, h, way, src=None):
            return pltpu.make_async_remote_copy(
                src_ref=self.piece(slot, h) if src is None else src,
                dst_ref=self.piece(slot, h),
                send_sem=w_send.at[self.m, way, slot * 2 + h],
                recv_sem=w_recv.at[self.m, slot * 2 + h],
                device_id=self.ways[way],
                device_id_type=MESH,
            )

        def wait(self, slot, h):
            self.copy(slot, h, 0).wait_recv()

        def pass_on(self, dp, dq, h, *ways):
            slot = self.slot(dp, dq)
            self.wait(slot, h)
            for way in ways:
                self.copy(slot, h, way).start()

    walks = (Walk(0), Walk(1))
    own_slot = walks[0].slot(0, 0)

    load_own = [
        pltpu.make_async_copy(
            w.own(h), w.piece(own_slot, h), local_sem.at[9 + 2 * w.m + h]
        )
        for h in range(2)
        for w in walks
    ]

    @pl.when(source)
    def _():
        for load in load_own:
            load.start()

    barrier = pltpu.get_barrier_semaphore()
    for there in plane:
        pl.semaphore_signal(
            barrier, inc=1, device_id=(there, t), device_id_type=MESH
        )
    for d in range(1, N_TOK):
        pl.semaphore_signal(
            barrier, inc=1, device_id=(g, (t + d) % N_TOK), device_id_type=MESH
        )
    pl.semaphore_wait(barrier, N_TOK + 3)

    @pl.when(source)
    def _():
        for i in range(4):
            load_own[i].wait()
            for way in range(4):
                walks[i % 2].copy(own_slot, i // 2, way).start()

    def near_first():
        @pl.when(relay)
        def _():
            for w in walks:
                w.pass_on(-1, 0, 0, P_NEXT, Q_NEXT, Q_PREV)
                w.pass_on(1, 0, 0, Q_NEXT, Q_PREV)
            for w in walks:
                w.pass_on(0, -1, 0, Q_NEXT)

    def near_second():
        @pl.when(relay)
        def _():
            for w in walks:
                w.pass_on(1, 0, 1, P_PREV, Q_NEXT, Q_PREV)
                w.pass_on(-1, 0, 1, Q_NEXT, Q_PREV)
            for w in walks:
                w.pass_on(0, 1, 1, Q_PREV)

    def far_half(h):
        @pl.when(source)
        def _():
            for w in walks:
                w.pass_on(2, 0, h, Q_NEXT, Q_PREV)

    def rows_first():
        for w in walks:
            @pl.when(source)
            def _(w=w):
                w.pass_on(-1, -1, 0, Q_NEXT)
                w.pass_on(1, -1, 0, Q_NEXT)

    def rows_far_first():
        for w in walks:
            @pl.when(relay)
            def _(w=w):
                w.pass_on(2, -1, 0, Q_NEXT)

    def rows_second():
        for w in walks:
            @pl.when(source)
            def _(w=w):
                w.pass_on(-1, 1, 1, Q_PREV)
                w.pass_on(1, 1, 1, Q_PREV)

    def rows_far_second():
        for w in walks:
            @pl.when(relay)
            def _(w=w):
                w.pass_on(2, 1, 1, Q_PREV)

    def ring(buf, send, recv, cols=None):
        def copy(slot, n_send, n_recv, there, part=None, src=None):
            ref = buf.at[slot]
            if part is not None:
                ref = ref.at[pl.ds(part * half, half)]
            if cols is not None:
                ref = ref.at[:, pl.ds(*cols)]
            return pltpu.make_async_remote_copy(
                src_ref=ref if src is None else src,
                dst_ref=ref,
                send_sem=send.at[n_send],
                recv_sem=recv.at[n_recv],
                device_id=there,
                device_id_type=MESH,
            )

        prev_s = wrap(x - 1) * 2 + c
        next_s = wrap(x + 1) * 2 + c
        far_s = wrap(x + 2) * 2 + c
        other = 1 - 2 * c

        def begin(src=None):
            copy(t, 0, 0, x_next, src=src).start()
            copy(t, 1, 1, x_prev, src=src).start()
            copy(t, 2, 4, sibling, src=src).start()

        def relay_near():
            copy(prev_s, 0, 0, x_next).wait_recv()
            copy(prev_s, 3, 2, x_next, part=0).start()
            copy(prev_s, 4, 5, sibling).start()
            copy(next_s, 1, 1, x_prev).wait_recv()
            copy(next_s, 5, 3, x_prev, part=1).start()
            copy(next_s, 6, 6, sibling).start()

        def relay_far():
            copy(far_s, 3, 2, x_next, part=0).wait_recv()
            copy(far_s, 7, 7, sibling, part=0).start()
            copy(far_s, 5, 3, x_prev, part=1).wait_recv()
            copy(far_s, 8, 8, sibling, part=1).start()

        def sibling_own():
            copy(t + other, 2, 4, sibling).wait_recv()

        def sibling_near():
            copy(prev_s + other, 4, 5, sibling).wait_recv()
            copy(next_s + other, 6, 6, sibling).wait_recv()

        def sibling_far():
            copy(far_s + other, 7, 7, sibling, part=0).wait_recv()
            copy(far_s + other, 8, 8, sibling, part=1).wait_recv()

        def drain():
            copy(t, 0, 0, x_next).wait_send()
            copy(t, 1, 1, x_prev).wait_send()
            copy(t, 2, 4, sibling).wait_send()
            copy(prev_s, 3, 2, x_next, part=0).wait_send()
            copy(prev_s, 4, 5, sibling).wait_send()
            copy(next_s, 5, 3, x_prev, part=1).wait_send()
            copy(next_s, 6, 6, sibling).wait_send()
            copy(far_s, 7, 7, sibling, part=0).wait_send()
            copy(far_s, 8, 8, sibling, part=1).wait_send()

        return (
            begin,
            relay_near,
            relay_far,
            sibling_own,
            sibling_near,
            sibling_far,
            drain,
        )

    kv_ring = ring(kvbuf, kv_send, kv_recv)
    kv_ring[0](kv_in)

    def seg_copy(d):
        return pltpu.make_async_remote_copy(
            src_ref=seg_in,
            dst_ref=segbuf.at[t],
            send_sem=seg_send,
            recv_sem=seg_recv,
            device_id=(g, (t + d) % N_TOK),
            device_id_type=MESH,
        )

    for d in range(1, N_TOK):
        seg_copy(d).start()

    load_kv = pltpu.make_async_copy(kv_in, kvbuf.at[t], local_sem.at[0])
    load_q = pltpu.make_async_copy(q_in, qbuf, local_sem.at[1])
    load_res = pltpu.make_async_copy(res_in, resbuf, local_sem.at[2])
    load_cache = pltpu.make_async_copy(cache_in, cachebuf, local_sem.at[3])
    load_seg = pltpu.make_async_copy(seg_in, segbuf.at[t], local_sem.at[4])
    load_kv.start()
    load_q.start()
    load_seg.start()
    load_res.start()
    load_cache.start()

    load_seg.wait()
    pltpu.make_async_copy(segbuf.at[pl.ds(0, N_TOK - 1)], segbuf.at[pl.ds(0, N_TOK - 1)], seg_recv).wait()
    own_seg = jnp.broadcast_to(seg_in[...], (rows, rows)).T
    row_id = lax.broadcasted_iota(jnp.int32, (rows, rows), 0) + t * rows
    col_id = lax.broadcasted_iota(jnp.int32, (rows, rows), 1)
    for i in range(N_TOK):
        live = (own_seg == segbuf[i]) & (col_id + i * rows <= row_id)
        biasbuf[:, i * rows : (i + 1) * rows] = jnp.where(live, 0.0, MASKED)

    kv_ring[1]()

    near_first()
    kv_ring[2]()
    load_kv.wait()
    load_q.wait()
    load_res.wait()
    kv_ring[3]()
    kv_ring[4]()
    kv_ring[5]()

    scale = 1.0 / math.sqrt(HEAD)

    def attend(h, squares):
        base = pl.multiple_of(h * (GROUP * HEAD), HEAD)
        queries = jnp.concatenate(
            [qbuf[:, pl.ds(base + j * HEAD, HEAD)] for j in range(GROUP)], axis=0
        )
        k_col = pl.multiple_of(h * HEAD, HEAD)
        k = kvbuf[:, :, pl.ds(k_col, HEAD)].reshape(keys, HEAD)
        v = kvbuf[:, :, pl.ds(k_col + KV_HEADS * HEAD, HEAD)].reshape(keys, HEAD)
        scores = lax.dot_general(
            queries, k, (((1,), (1,)), ((), ())), preferred_element_type=jnp.float32
        )
        scores = scores.reshape(GROUP, rows, keys) + biasbuf[...][None]
        top = jnp.max(scores, axis=-1, keepdims=True)
        weights = jnp.exp((scores - top) * scale)
        total = jnp.sum(weights, axis=-1, keepdims=True)
        weights = weights.astype(jnp.bfloat16).reshape(GROUP * rows, keys)
        out = jnp.dot(weights, v, preferred_element_type=jnp.float32)
        out = (out.reshape(GROUP, rows, HEAD) / total).astype(jnp.bfloat16)
        for j in range(GROUP):
            cols = pl.ds(base + j * HEAD, HEAD)
            a = resbuf[:, cols].astype(jnp.float32) + out[j].astype(jnp.float32)
            a = a.astype(jnp.bfloat16)
            attbuf[:, cols] = a
            a = a.astype(jnp.float32)
            normbuf[t, :, cols] = (a * gain_in[:, cols]).astype(jnp.bfloat16)
            squares = squares + a * a
        return squares

    width = 2 * GROUP * HEAD
    rings = [
        ring(normbuf, nrm_send.at[i], nrm_recv.at[i], (i * width, width))
        for i in range(KV_HEADS // 2)
    ]
    squares = jnp.zeros((rows, HEAD), jnp.float32)
    squares = lax.fori_loop(0, 2, attend, squares)
    rings[0][0]()
    far_half(0)
    squares = lax.fori_loop(2, 4, attend, squares)
    rings[1][0]()
    near_second()
    squares = lax.fori_loop(4, 6, attend, squares)
    rings[2][0]()
    rings[0][1]()
    squares = lax.fori_loop(6, 8, attend, squares)
    rings[3][0]()
    mean = jnp.sum(squares, axis=-1, keepdims=True) * (1.0 / WIDTH)
    inverse = jnp.broadcast_to(lax.rsqrt(mean + 1e-6), (rows, rows))
    scalebuf[t] = inverse
    statbuf[t] = inverse.T[:1]

    def stat_copy(d):
        return pltpu.make_async_remote_copy(
            src_ref=statbuf.at[t],
            dst_ref=statbuf.at[t],
            send_sem=stat_send,
            recv_sem=stat_recv,
            device_id=(g, (t + d) % N_TOK),
            device_id_type=MESH,
        )

    for d in range(1, N_TOK):
        stat_copy(d).start()
    store_att = pltpu.make_async_copy(attbuf, att_out, local_sem.at[7])
    store_att.start()
    far_half(1)
    rings[0][2]()
    rows_first()
    rings[1][1]()

    load_cache.wait()
    table = jnp.broadcast_to(table_in[...], (8, table_in.shape[1]))
    page_id = lax.broadcasted_iota(jnp.int32, (table_in.shape[1], keys), 0)
    key_id = lax.broadcasted_iota(jnp.int32, (table_in.shape[1], keys), 1)
    spread = (page_id == key_id // PAGE).astype(jnp.float32).astype(jnp.bfloat16)
    slot_of = jnp.dot(
        table.astype(jnp.float32).astype(jnp.bfloat16),
        spread,
        preferred_element_type=jnp.float32,
    )
    key_row = lax.broadcasted_iota(jnp.int32, (8, keys), 1)
    key_row = (key_row % PAGE).astype(jnp.float32)
    shift = (t * slots_here).astype(jnp.float32)
    goal = ((slot_of - shift) * PAGE + key_row)[:1]
    here = lax.broadcasted_iota(jnp.int32, (slots_here * PAGE, keys), 0)
    picked = (here.astype(jnp.float32) == goal).astype(jnp.float32)
    covered = jnp.sum(picked, axis=-1, keepdims=True) > 0.5
    picked = picked.astype(jnp.bfloat16)
    chunk = 512

    def place(i, carry):
        cols = pl.ds(pl.multiple_of(i * chunk, chunk), chunk)
        rows_kv = kvbuf[:, :, cols].reshape(keys, chunk)
        new = jnp.dot(picked, rows_kv, preferred_element_type=jnp.float32)
        old = cachebuf[:, :, cols].reshape(slots_here * PAGE, chunk)
        both = jnp.where(covered, new, old.astype(jnp.float32)).astype(jnp.bfloat16)
        placedbuf[:, :, cols] = both.reshape(slots_here, PAGE, chunk)
        return carry

    lax.fori_loop(0, kv_in.shape[1] // chunk, place, 0)
    store_cache = pltpu.make_async_copy(placedbuf, cache_out, local_sem.at[8])
    store_cache.start()

    rows_far_first()
    rings[1][2]()
    rings[2][1]()
    rows_second()
    rings[2][2]()
    rings[3][1]()
    some = statbuf.at[pl.ds(0, N_TOK - 1)]
    pltpu.make_async_copy(some, some, stat_recv).wait()

    def spread_scale(d, carry):
        there = (t + d) % N_TOK
        scalebuf[there] = jnp.broadcast_to(statbuf[there], (rows, rows)).T
        return carry

    lax.fori_loop(1, N_TOK, spread_scale, 0)
    rows_far_second()
    rings[3][2]()
    for part in rings:
        part[3]()
        part[4]()
        part[5]()

    parts = 2
    per = N_TOK // parts

    def choose(i, values):
        out = jnp.int32(values[-1])
        for k in range(len(values) - 1):
            out = jnp.where(i == k, values[k], out)
        return out

    def project(i, carry):
        dz = jnp.where(
            source,
            choose(i, (0, 2, 0, 1, 1, 3, 3, 2)),
            choose(i, (1, 3, 0, 0, 3, 2, 1, 2)),
        )
        dy = jnp.where(
            source,
            choose(i, (0, 0, 2, 1, 3, 1, 3, 2)),
            choose(i, (0, 0, 1, 3, 2, 3, 2, 1)),
        )
        zz, yy = wrap(z + dz), wrap(y + dy)
        slot = yy * 2 + zz // 2
        for w in walks:
            dq = jnp.where(w.z_first, dy, dz)

            @pl.when((dq == 1) | (dq == 2))
            def _(w=w):
                w.wait(slot, 0)

            @pl.when((dq == 3) | (dq == 2))
            def _(w=w):
                w.wait(slot, 1)

        column = pl.multiple_of(grp_of(zz, yy) * units + x_col, COLS)

        def tile(k, carry):
            some = pl.ds(k * per, per)
            tokens = normbuf[some].reshape(per * rows, WIDTH)
            both = jnp.concatenate([wbuf[slot, 0], wbuf[slot, 1]], axis=1)
            sums = jnp.dot(tokens, both, preferred_element_type=jnp.float32)
            scale = scalebuf[some].reshape(per * rows, COLS)
            gate, up = sums[:, :COLS] * scale, sums[:, COLS:] * scale
            value = gate / (1.0 + jnp.exp(-gate)) * up
            hidbuf[slot, some] = value.astype(jnp.bfloat16).reshape(per, rows, COLS)
            return carry

        lax.fori_loop(0, parts, tile, 0)
        pltpu.make_async_copy(
            hidbuf.at[slot, t], hid_out.at[:, pl.ds(column, COLS)], hid_recv
        ).start()

        def send(d, carry):
            there = (t + d) % N_TOK
            pltpu.make_async_remote_copy(
                src_ref=hidbuf.at[slot, there],
                dst_ref=hid_out.at[:, pl.ds(column, COLS)],
                send_sem=hid_send,
                recv_sem=hid_recv,
                device_id=(g, there),
                device_id_type=MESH,
            ).start()
            return carry

        lax.fori_loop(1, N_TOK, send, 0)
        return carry

    lax.fori_loop(0, 8, project, 0)

    store_att.wait()
    store_cache.wait()
    pltpu.make_async_copy(
        segbuf.at[pl.ds(0, N_TOK - 1)], segbuf.at[pl.ds(0, N_TOK - 1)], seg_send
    ).wait()
    kv_ring[6]()
    pltpu.make_async_copy(some, some, stat_send).wait()
    for part in rings:
        part[6]()

    @pl.when(source)
    def _():
        for w in walks:
            for h in range(2):
                for way in range(4):
                    w.copy(own_slot, h, way).wait_send()
                w.copy(w.slot(2, 0), h, Q_NEXT).wait_send()
                w.copy(w.slot(2, 0), h, Q_PREV).wait_send()
            for dp in (-1, 1):
                w.copy(w.slot(dp, -1), 0, Q_NEXT).wait_send()
                w.copy(w.slot(dp, 1), 1, Q_PREV).wait_send()

    @pl.when(relay)
    def _():
        for w in walks:
            w.copy(w.slot(-1, 0), 0, P_NEXT).wait_send()
            w.copy(w.slot(1, 0), 1, P_PREV).wait_send()
            for h in range(2):
                for dp in (-1, 1):
                    w.copy(w.slot(dp, 0), h, Q_NEXT).wait_send()
                    w.copy(w.slot(dp, 0), h, Q_PREV).wait_send()
            for dp in (0, 2):
                w.copy(w.slot(dp, -1), 0, Q_NEXT).wait_send()
                w.copy(w.slot(dp, 1), 1, Q_PREV).wait_send()

    whole = hidbuf.at[:, pl.ds(0, N_TOK - 1)]
    pltpu.make_async_copy(whole, whole, hid_send).wait()
    pltpu.make_async_copy(hidbuf, hidbuf, hid_recv).wait()


def on_device(
    queries,
    rotated_keys_values,
    prompt_window_index,
    residual,
    ffn_gain,
    gate_weight,
    up_weight,
    paged_cache,
    page_table,
):
    rows = queries.shape[0]
    kv_width = rotated_keys_values.shape[1]
    hidden_width = gate_weight.shape[1] * SIDE * SIDE
    any_space = pl.BlockSpec(memory_space=pl.ANY)
    vmem = pl.BlockSpec(memory_space=pltpu.VMEM)
    bf16 = jnp.bfloat16
    dma = pltpu.SemaphoreType.DMA
    outs = pl.pallas_call(
        kernel,
        out_shape=(
            jax.ShapeDtypeStruct(residual.shape, bf16),
            jax.ShapeDtypeStruct((rows, hidden_width), bf16),
            jax.ShapeDtypeStruct(paged_cache.shape, bf16),
        ),
        in_specs=[
            any_space,
            any_space,
            vmem,
            any_space,
            vmem,
            any_space,
            any_space,
            any_space,
            vmem,
        ],
        out_specs=(any_space, any_space, any_space),
        scratch_shapes=[
            pltpu.VMEM(queries.shape, bf16),
            pltpu.VMEM((N_TOK, rows, kv_width), bf16),
            pltpu.VMEM((N_TOK, 1, rows), jnp.int32),
            pltpu.VMEM(residual.shape, bf16),
            pltpu.VMEM(paged_cache.shape, bf16),
            pltpu.VMEM(paged_cache.shape, bf16),
            pltpu.VMEM(residual.shape, bf16),
            pltpu.VMEM((rows, N_TOK * rows), jnp.float32),
            pltpu.VMEM((N_TOK, 1, rows), jnp.float32),
            pltpu.VMEM((N_TOK, rows, COLS), jnp.float32),
            pltpu.VMEM((N_TOK, rows, WIDTH), bf16),
            pltpu.VMEM((8, 2, WIDTH, COLS), bf16),
            pltpu.VMEM((8, N_TOK, rows, COLS), bf16),
            dma((9,)),
            dma((9,)),
            dma((KV_HEADS // 2, 9)),
            dma((KV_HEADS // 2, 9)),
            dma((2, 4, 16)),
            dma((2, 16)),
            dma(()),
            dma(()),
            dma(()),
            dma(()),
            dma(()),
            dma(()),
            dma((13,)),
        ],
        compiler_params=pltpu.CompilerParams(
            collective_id=0,
            has_side_effects=True,
            vmem_limit_bytes=63 * 1024 * 1024,
        ),
        name="layer",
    )(
        queries,
        rotated_keys_values,
        prompt_window_index,
        residual,
        ffn_gain.reshape(1, -1),
        gate_weight,
        up_weight,
        paged_cache,
        page_table,
    )
    return tuple(outs)


def solution(mesh):
    in_specs = (
        P(("grp", "tok"), None),
        P(("grp", "tok"), None),
        P("grp", "tok"),
        P(("grp", "tok"), None),
        P(),
        P(None, "grp"),
        P(None, "grp"),
        P(("grp", "tok"), None, None),
        P("grp", None),
    )
    out_specs = (P(("grp", "tok"), None), P(("grp", "tok"), None), P(("grp", "tok"), None, None))
    return jax.shard_map(
        on_device, mesh=mesh, in_specs=in_specs, out_specs=out_specs, check_vma=False
    )
```

```python
import math

import jax
import jax.numpy as jnp
from jax import lax
from jax.experimental import pallas as pl
from jax.experimental.pallas import tpu as pltpu
from jax.sharding import PartitionSpec as P

HEADS = 40
KV_HEADS = 8
HEAD = 128
GROUP = HEADS // KV_HEADS
PAGE = 16
WIDTH = HEADS * HEAD
COLS = 128
SIDE = 4
N_TOK = 8
MASKED = -1e30
MESH = pl.DeviceIdType.MESH


def kernel(
    q_in,
    kv_in,
    seg_in,
    res_in,
    gain_in,
    gate_in,
    up_in,
    cache_in,
    table_in,
    att_out,
    hid_out,
    cache_out,
    qbuf,
    kvbuf,
    segbuf,
    resbuf,
    cachebuf,
    biasbuf,
    statbuf,
    scalebuf,
    normbuf,
    wbuf,
    hidbuf,
    kv_send,
    kv_recv,
    nrm_send,
    nrm_recv,
    w_send,
    w_recv,
    seg_send,
    seg_recv,
    stat_send,
    stat_recv,
    hid_send,
    hid_recv,
    local_sem,
):
    rows = q_in.shape[0]
    half = rows // 2
    keys = N_TOK * rows
    slots_here = cache_in.shape[0]
    units = gate_in.shape[1]
    g = lax.axis_index("grp")
    t = lax.axis_index("tok")
    x, c = t // 2, t % 2
    z, y = g // SIDE, g % SIDE
    def wrap(v):
        return (v + SIDE) % SIDE

    def grp_of(zz, yy):
        return zz * SIDE + yy

    x_next = (g, wrap(x + 1) * 2 + c)
    x_prev = (g, wrap(x - 1) * 2 + c)
    sibling = (g, x * 2 + 1 - c)
    plane = (
        grp_of(wrap(z + 1), y),
        grp_of(wrap(z - 1), y),
        grp_of(z, wrap(y + 1)),
        grp_of(z, wrap(y - 1)),
    )
    P_NEXT, P_PREV, Q_NEXT, Q_PREV = 0, 1, 2, 3

    source = (z + y) % 2 == c
    relay = jnp.logical_not(source)
    x_col = pl.multiple_of(x * COLS, COLS)
    deep = WIDTH // 2

    class Walk:
        def __init__(self, m):
            self.m = m
            self.z_first = c == m
            self.p = jnp.where(self.z_first, z, y)
            self.q = jnp.where(self.z_first, y, z)
            z_ways, y_ways = plane[:2], plane[2:]
            self.ways = [
                (jnp.where(self.z_first, a, b), t)
                for a, b in zip(z_ways + y_ways, y_ways + z_ways)
            ]

        def slot(self, dp, dq):
            pp, qq = wrap(self.p + dp), wrap(self.q + dq)
            zz = jnp.where(self.z_first, pp, qq)
            yy = jnp.where(self.z_first, qq, pp)
            return yy * 2 + zz // 2

        def own(self, h):
            ref = (gate_in, up_in)[self.m]
            return ref.at[pl.ds(h * deep, deep), pl.ds(x_col, COLS)]

        def piece(self, slot, h):
            return wbuf.at[slot, self.m, pl.ds(h * deep, deep)]

        def copy(self, slot, h, way, src=None):
            return pltpu.make_async_remote_copy(
                src_ref=self.piece(slot, h) if src is None else src,
                dst_ref=self.piece(slot, h),
                send_sem=w_send.at[self.m, way, slot * 2 + h],
                recv_sem=w_recv.at[self.m, slot * 2 + h],
                device_id=self.ways[way],
                device_id_type=MESH,
            )

        def wait(self, slot, h):
            self.copy(slot, h, 0).wait_recv()

        def pass_on(self, dp, dq, h, *ways):
            slot = self.slot(dp, dq)
            self.wait(slot, h)
            for way in ways:
                self.copy(slot, h, way).start()

    walks = (Walk(0), Walk(1))
    own_slot = walks[0].slot(0, 0)

    load_own = [
        pltpu.make_async_copy(
            w.own(h), w.piece(own_slot, h), local_sem.at[9 + 2 * w.m + h]
        )
        for h in range(2)
        for w in walks
    ]

    @pl.when(source)
    def _():
        for load in load_own:
            load.start()

    barrier = pltpu.get_barrier_semaphore()
    for there in plane:
        pl.semaphore_signal(
            barrier, inc=1, device_id=(there, t), device_id_type=MESH
        )
    for d in range(1, N_TOK):
        pl.semaphore_signal(
            barrier, inc=1, device_id=(g, (t + d) % N_TOK), device_id_type=MESH
        )
    pl.semaphore_wait(barrier, N_TOK + 3)

    @pl.when(source)
    def _():
        for i in range(4):
            load_own[i].wait()
            for way in range(4):
                walks[i % 2].copy(own_slot, i // 2, way).start()

    def near_first():
        @pl.when(relay)
        def _():
            for w in walks:
                w.pass_on(-1, 0, 0, P_NEXT, Q_NEXT, Q_PREV)
                w.pass_on(1, 0, 0, Q_NEXT, Q_PREV)
            for w in walks:
                w.pass_on(0, -1, 0, Q_NEXT)

    def near_second():
        @pl.when(relay)
        def _():
            for w in walks:
                w.pass_on(1, 0, 1, P_PREV, Q_NEXT, Q_PREV)
                w.pass_on(-1, 0, 1, Q_NEXT, Q_PREV)
            for w in walks:
                w.pass_on(0, 1, 1, Q_PREV)

    def far_half(h):
        @pl.when(source)
        def _():
            for w in walks:
                w.pass_on(2, 0, h, Q_NEXT, Q_PREV)

    def rows_first():
        for w in walks:
            @pl.when(source)
            def _(w=w):
                w.pass_on(-1, -1, 0, Q_NEXT)
                w.pass_on(1, -1, 0, Q_NEXT)

    def rows_far_first():
        for w in walks:
            @pl.when(relay)
            def _(w=w):
                w.pass_on(2, -1, 0, Q_NEXT)

    def rows_second():
        for w in walks:
            @pl.when(source)
            def _(w=w):
                w.pass_on(-1, 1, 1, Q_PREV)
                w.pass_on(1, 1, 1, Q_PREV)

    def rows_far_second():
        for w in walks:
            @pl.when(relay)
            def _(w=w):
                w.pass_on(2, 1, 1, Q_PREV)

    def ring(buf, send, recv, cols=None):
        def copy(slot, n_send, n_recv, there, part=None, src=None):
            ref = buf.at[slot]
            if part is not None:
                ref = ref.at[pl.ds(part * half, half)]
            if cols is not None:
                ref = ref.at[:, pl.ds(*cols)]
            return pltpu.make_async_remote_copy(
                src_ref=ref if src is None else src,
                dst_ref=ref,
                send_sem=send.at[n_send],
                recv_sem=recv.at[n_recv],
                device_id=there,
                device_id_type=MESH,
            )

        prev_s = wrap(x - 1) * 2 + c
        next_s = wrap(x + 1) * 2 + c
        far_s = wrap(x + 2) * 2 + c
        other = 1 - 2 * c

        def begin(src=None):
            copy(t, 0, 0, x_next, src=src).start()
            copy(t, 1, 1, x_prev, src=src).start()
            copy(t, 2, 4, sibling, src=src).start()

        def relay_near():
            copy(prev_s, 0, 0, x_next).wait_recv()
            copy(prev_s, 3, 2, x_next, part=0).start()
            copy(prev_s, 4, 5, sibling).start()
            copy(next_s, 1, 1, x_prev).wait_recv()
            copy(next_s, 5, 3, x_prev, part=1).start()
            copy(next_s, 6, 6, sibling).start()

        def relay_far():
            copy(far_s, 3, 2, x_next, part=0).wait_recv()
            copy(far_s, 7, 7, sibling, part=0).start()
            copy(far_s, 5, 3, x_prev, part=1).wait_recv()
            copy(far_s, 8, 8, sibling, part=1).start()

        def sibling_own():
            copy(t + other, 2, 4, sibling).wait_recv()

        def sibling_near():
            copy(prev_s + other, 4, 5, sibling).wait_recv()
            copy(next_s + other, 6, 6, sibling).wait_recv()

        def sibling_far():
            copy(far_s + other, 7, 7, sibling, part=0).wait_recv()
            copy(far_s + other, 8, 8, sibling, part=1).wait_recv()

        def drain():
            copy(t, 0, 0, x_next).wait_send()
            copy(t, 1, 1, x_prev).wait_send()
            copy(t, 2, 4, sibling).wait_send()
            copy(prev_s, 3, 2, x_next, part=0).wait_send()
            copy(prev_s, 4, 5, sibling).wait_send()
            copy(next_s, 5, 3, x_prev, part=1).wait_send()
            copy(next_s, 6, 6, sibling).wait_send()
            copy(far_s, 7, 7, sibling, part=0).wait_send()
            copy(far_s, 8, 8, sibling, part=1).wait_send()

        return (
            begin,
            relay_near,
            relay_far,
            sibling_own,
            sibling_near,
            sibling_far,
            drain,
        )

    kv_ring = ring(kvbuf, kv_send, kv_recv)
    kv_ring[0](kv_in)

    def seg_copy(d):
        return pltpu.make_async_remote_copy(
            src_ref=seg_in,
            dst_ref=segbuf.at[t],
            send_sem=seg_send,
            recv_sem=seg_recv,
            device_id=(g, (t + d) % N_TOK),
            device_id_type=MESH,
        )

    for d in range(1, N_TOK):
        seg_copy(d).start()

    load_kv = pltpu.make_async_copy(kv_in, kvbuf.at[t], local_sem.at[0])
    load_q = pltpu.make_async_copy(q_in, qbuf, local_sem.at[1])
    load_res = pltpu.make_async_copy(res_in, resbuf, local_sem.at[2])
    load_cache = pltpu.make_async_copy(cache_in, cachebuf, local_sem.at[3])
    load_seg = pltpu.make_async_copy(seg_in, segbuf.at[t], local_sem.at[4])
    load_kv.start()
    load_q.start()
    load_seg.start()
    load_res.start()
    load_cache.start()

    load_seg.wait()
    pltpu.make_async_copy(segbuf.at[pl.ds(0, N_TOK - 1)], segbuf.at[pl.ds(0, N_TOK - 1)], seg_recv).wait()
    own_seg = jnp.broadcast_to(seg_in[...], (rows, rows)).T
    row_id = lax.broadcasted_iota(jnp.int32, (rows, rows), 0) + t * rows
    col_id = lax.broadcasted_iota(jnp.int32, (rows, rows), 1)
    for i in range(N_TOK):
        live = (own_seg == segbuf[i]) & (col_id + i * rows <= row_id)
        biasbuf[:, i * rows : (i + 1) * rows] = jnp.where(live, 0.0, MASKED)

    kv_ring[1]()

    near_first()
    kv_ring[2]()
    load_kv.wait()
    load_q.wait()
    load_res.wait()
    kv_ring[3]()
    kv_ring[4]()
    kv_ring[5]()

    scale = 1.0 / math.sqrt(HEAD)

    def attend(h, squares):
        base = pl.multiple_of(h * (GROUP * HEAD), HEAD)
        queries = jnp.concatenate(
            [qbuf[:, pl.ds(base + j * HEAD, HEAD)] for j in range(GROUP)], axis=0
        )
        k_col = pl.multiple_of(h * HEAD, HEAD)
        k = kvbuf[:, :, pl.ds(k_col, HEAD)].reshape(keys, HEAD)
        v = kvbuf[:, :, pl.ds(k_col + KV_HEADS * HEAD, HEAD)].reshape(keys, HEAD)
        scores = lax.dot_general(
            queries, k, (((1,), (1,)), ((), ())), preferred_element_type=jnp.float32
        )
        scores = scores.reshape(GROUP, rows, keys) + biasbuf[...][None]
        top = jnp.max(scores, axis=-1, keepdims=True)
        weights = jnp.exp((scores - top) * scale)
        total = jnp.sum(weights, axis=-1, keepdims=True)
        weights = weights.astype(jnp.bfloat16).reshape(GROUP * rows, keys)
        out = jnp.dot(weights, v, preferred_element_type=jnp.float32)
        out = (out.reshape(GROUP, rows, HEAD) / total).astype(jnp.bfloat16)
        for j in range(GROUP):
            cols = pl.ds(base + j * HEAD, HEAD)
            a = resbuf[:, cols].astype(jnp.float32) + out[j].astype(jnp.float32)
            a = a.astype(jnp.bfloat16)
            att_out[:, cols] = a
            a = a.astype(jnp.float32)
            normbuf[t, :, cols] = (a * gain_in[:, cols]).astype(jnp.bfloat16)
            squares = squares + a * a
        return squares

    width = 2 * GROUP * HEAD
    rings = [
        ring(normbuf, nrm_send.at[i], nrm_recv.at[i], (i * width, width))
        for i in range(KV_HEADS // 2)
    ]
    squares = jnp.zeros((rows, HEAD), jnp.float32)
    squares = lax.fori_loop(0, 2, attend, squares)
    rings[0][0]()
    far_half(0)
    squares = lax.fori_loop(2, 4, attend, squares)
    rings[1][0]()
    near_second()
    squares = lax.fori_loop(4, 6, attend, squares)
    rings[2][0]()
    rings[0][1]()
    squares = lax.fori_loop(6, 8, attend, squares)
    rings[3][0]()
    mean = jnp.sum(squares, axis=-1, keepdims=True) * (1.0 / WIDTH)
    inverse = jnp.broadcast_to(lax.rsqrt(mean + 1e-6), (rows, rows))
    scalebuf[t] = inverse
    statbuf[t] = inverse.T[:1]

    def stat_copy(d):
        return pltpu.make_async_remote_copy(
            src_ref=statbuf.at[t],
            dst_ref=statbuf.at[t],
            send_sem=stat_send,
            recv_sem=stat_recv,
            device_id=(g, (t + d) % N_TOK),
            device_id_type=MESH,
        )

    for d in range(1, N_TOK):
        stat_copy(d).start()
    far_half(1)
    rings[0][2]()
    rows_first()
    rings[1][1]()

    load_cache.wait()
    table = jnp.broadcast_to(table_in[...], (8, table_in.shape[1]))
    page_id = lax.broadcasted_iota(jnp.int32, (table_in.shape[1], keys), 0)
    key_id = lax.broadcasted_iota(jnp.int32, (table_in.shape[1], keys), 1)
    spread = (page_id == key_id // PAGE).astype(jnp.float32).astype(jnp.bfloat16)
    slot_of = jnp.dot(
        table.astype(jnp.float32).astype(jnp.bfloat16),
        spread,
        preferred_element_type=jnp.float32,
    )
    key_row = lax.broadcasted_iota(jnp.int32, (8, keys), 1)
    key_row = (key_row % PAGE).astype(jnp.float32)
    shift = (t * slots_here).astype(jnp.float32)
    goal = ((slot_of - shift) * PAGE + key_row)[:1]
    here = lax.broadcasted_iota(jnp.int32, (slots_here * PAGE, keys), 0)
    picked = (here.astype(jnp.float32) == goal).astype(jnp.float32)
    covered = jnp.sum(picked, axis=-1, keepdims=True) > 0.5
    picked = picked.astype(jnp.bfloat16)
    chunk = 512

    def place(i, carry):
        cols = pl.ds(pl.multiple_of(i * chunk, chunk), chunk)
        rows_kv = kvbuf[:, :, cols].reshape(keys, chunk)
        new = jnp.dot(picked, rows_kv, preferred_element_type=jnp.float32)
        old = cachebuf[:, :, cols].reshape(slots_here * PAGE, chunk)
        both = jnp.where(covered, new, old.astype(jnp.float32)).astype(jnp.bfloat16)
        cache_out[:, :, cols] = both.reshape(slots_here, PAGE, chunk)
        return carry

    lax.fori_loop(0, kv_in.shape[1] // chunk, place, 0)

    rows_far_first()
    rings[1][2]()
    rings[2][1]()
    rows_second()
    rings[2][2]()
    rings[3][1]()
    some = statbuf.at[pl.ds(0, N_TOK - 1)]
    pltpu.make_async_copy(some, some, stat_recv).wait()

    def spread_scale(d, carry):
        there = (t + d) % N_TOK
        scalebuf[there] = jnp.broadcast_to(statbuf[there], (rows, rows)).T
        return carry

    lax.fori_loop(1, N_TOK, spread_scale, 0)
    rows_far_second()
    rings[3][2]()
    for part in rings:
        part[3]()
        part[4]()
        part[5]()

    parts = 2
    per = N_TOK // parts

    def choose(i, values):
        out = jnp.int32(values[-1])
        for k in range(len(values) - 1):
            out = jnp.where(i == k, values[k], out)
        return out

    def project(i, carry):
        dz = jnp.where(
            source,
            choose(i, (0, 2, 0, 1, 1, 3, 3, 2)),
            choose(i, (1, 3, 0, 0, 3, 2, 1, 2)),
        )
        dy = jnp.where(
            source,
            choose(i, (0, 0, 2, 1, 3, 1, 3, 2)),
            choose(i, (0, 0, 1, 3, 2, 3, 2, 1)),
        )
        zz, yy = wrap(z + dz), wrap(y + dy)
        slot = yy * 2 + zz // 2
        for w in walks:
            dq = jnp.where(w.z_first, dy, dz)

            @pl.when((dq == 1) | (dq == 2))
            def _(w=w):
                w.wait(slot, 0)

            @pl.when((dq == 3) | (dq == 2))
            def _(w=w):
                w.wait(slot, 1)

        column = pl.multiple_of(grp_of(zz, yy) * units + x_col, COLS)

        def tile(k, carry):
            some = pl.ds(k * per, per)
            tokens = normbuf[some].reshape(per * rows, WIDTH)
            both = jnp.concatenate([wbuf[slot, 0], wbuf[slot, 1]], axis=1)
            sums = jnp.dot(tokens, both, preferred_element_type=jnp.float32)
            scale = scalebuf[some].reshape(per * rows, COLS)
            gate, up = sums[:, :COLS] * scale, sums[:, COLS:] * scale
            value = gate / (1.0 + jnp.exp(-gate)) * up
            hidbuf[slot, some] = value.astype(jnp.bfloat16).reshape(per, rows, COLS)
            return carry

        lax.fori_loop(0, parts, tile, 0)
        pltpu.make_async_copy(
            hidbuf.at[slot, t], hid_out.at[:, pl.ds(column, COLS)], hid_recv
        ).start()

        def send(d, carry):
            there = (t + d) % N_TOK
            pltpu.make_async_remote_copy(
                src_ref=hidbuf.at[slot, there],
                dst_ref=hid_out.at[:, pl.ds(column, COLS)],
                send_sem=hid_send,
                recv_sem=hid_recv,
                device_id=(g, there),
                device_id_type=MESH,
            ).start()
            return carry

        lax.fori_loop(1, N_TOK, send, 0)
        return carry

    lax.fori_loop(0, 8, project, 0)

    pltpu.make_async_copy(
        segbuf.at[pl.ds(0, N_TOK - 1)], segbuf.at[pl.ds(0, N_TOK - 1)], seg_send
    ).wait()
    kv_ring[6]()
    pltpu.make_async_copy(some, some, stat_send).wait()
    for part in rings:
        part[6]()

    @pl.when(source)
    def _():
        for w in walks:
            for h in range(2):
                for way in range(4):
                    w.copy(own_slot, h, way).wait_send()
                w.copy(w.slot(2, 0), h, Q_NEXT).wait_send()
                w.copy(w.slot(2, 0), h, Q_PREV).wait_send()
            for dp in (-1, 1):
                w.copy(w.slot(dp, -1), 0, Q_NEXT).wait_send()
                w.copy(w.slot(dp, 1), 1, Q_PREV).wait_send()

    @pl.when(relay)
    def _():
        for w in walks:
            w.copy(w.slot(-1, 0), 0, P_NEXT).wait_send()
            w.copy(w.slot(1, 0), 1, P_PREV).wait_send()
            for h in range(2):
                for dp in (-1, 1):
                    w.copy(w.slot(dp, 0), h, Q_NEXT).wait_send()
                    w.copy(w.slot(dp, 0), h, Q_PREV).wait_send()
            for dp in (0, 2):
                w.copy(w.slot(dp, -1), 0, Q_NEXT).wait_send()
                w.copy(w.slot(dp, 1), 1, Q_PREV).wait_send()

    whole = hidbuf.at[:, pl.ds(0, N_TOK - 1)]
    pltpu.make_async_copy(whole, whole, hid_send).wait()
    pltpu.make_async_copy(hidbuf, hidbuf, hid_recv).wait()


def on_device(
    queries,
    rotated_keys_values,
    prompt_window_index,
    residual,
    ffn_gain,
    gate_weight,
    up_weight,
    paged_cache,
    page_table,
):
    rows = queries.shape[0]
    kv_width = rotated_keys_values.shape[1]
    hidden_width = gate_weight.shape[1] * SIDE * SIDE
    any_space = pl.BlockSpec(memory_space=pl.ANY)
    vmem = pl.BlockSpec(memory_space=pltpu.VMEM)
    bf16 = jnp.bfloat16
    dma = pltpu.SemaphoreType.DMA
    outs = pl.pallas_call(
        kernel,
        out_shape=(
            pltpu.VMEM(residual.shape, bf16),
            pltpu.VMEM((rows, hidden_width), bf16),
            pltpu.VMEM(paged_cache.shape, bf16),
        ),
        in_specs=[
            any_space,
            any_space,
            vmem,
            any_space,
            vmem,
            any_space,
            any_space,
            any_space,
            vmem,
        ],
        out_specs=(vmem, vmem, vmem),
        scratch_shapes=[
            pltpu.VMEM(queries.shape, bf16),
            pltpu.VMEM((N_TOK, rows, kv_width), bf16),
            pltpu.VMEM((N_TOK, 1, rows), jnp.int32),
            pltpu.VMEM(residual.shape, bf16),
            pltpu.VMEM(paged_cache.shape, bf16),
            pltpu.VMEM((rows, N_TOK * rows), jnp.float32),
            pltpu.VMEM((N_TOK, 1, rows), jnp.float32),
            pltpu.VMEM((N_TOK, rows, COLS), jnp.float32),
            pltpu.VMEM((N_TOK, rows, WIDTH), bf16),
            pltpu.VMEM((8, 2, WIDTH, COLS), bf16),
            pltpu.VMEM((8, N_TOK, rows, COLS), bf16),
            dma((9,)),
            dma((9,)),
            dma((KV_HEADS // 2, 9)),
            dma((KV_HEADS // 2, 9)),
            dma((2, 4, 16)),
            dma((2, 16)),
            dma(()),
            dma(()),
            dma(()),
            dma(()),
            dma(()),
            dma(()),
            dma((13,)),
        ],
        compiler_params=pltpu.CompilerParams(
            collective_id=0,
            has_side_effects=True,
            vmem_limit_bytes=50 * 1024 * 1024,
        ),
        name="layer",
    )(
        queries,
        rotated_keys_values,
        prompt_window_index,
        residual,
        ffn_gain.reshape(1, -1),
        gate_weight,
        up_weight,
        paged_cache,
        page_table,
    )
    return tuple(outs)


def solution(mesh):
    in_specs = (
        P(("grp", "tok"), None),
        P(("grp", "tok"), None),
        P("grp", "tok"),
        P(("grp", "tok"), None),
        P(),
        P(None, "grp"),
        P(None, "grp"),
        P(("grp", "tok"), None, None),
        P("grp", None),
    )
    out_specs = (P(("grp", "tok"), None), P(("grp", "tok"), None), P(("grp", "tok"), None, None))
    return jax.shard_map(
        on_device, mesh=mesh, in_specs=in_specs, out_specs=out_specs, check_vma=False
    )
```

```python
import math

import jax
import jax.numpy as jnp
from jax import lax
from jax.experimental import pallas as pl
from jax.experimental.pallas import tpu as pltpu
from jax.sharding import PartitionSpec as P

HEADS = 40
KV_HEADS = 8
HEAD = 128
GROUP = HEADS // KV_HEADS
PAGE = 16
WIDTH = HEADS * HEAD
COLS = 128
SIDE = 4
N_TOK = 8
MASKED = -1e30
MESH = pl.DeviceIdType.MESH


def kernel(
    q_in,
    kv_in,
    seg_in,
    res_in,
    gain_in,
    gate_in,
    up_in,
    cache_in,
    table_in,
    att_out,
    hid_out,
    cache_out,
    qbuf,
    kvbuf,
    segbuf,
    resbuf,
    cachebuf,
    biasbuf,
    statbuf,
    scalebuf,
    normbuf,
    wbuf,
    hidbuf,
    kv_send,
    kv_recv,
    nrm_send,
    nrm_recv,
    w_send,
    w_recv,
    seg_send,
    seg_recv,
    stat_send,
    stat_recv,
    hid_send,
    hid_recv,
    local_sem,
):
    rows = q_in.shape[0]
    half = rows // 2
    keys = N_TOK * rows
    slots_here = cache_in.shape[0]
    units = gate_in.shape[1]
    g = lax.axis_index("grp")
    t = lax.axis_index("tok")
    x, c = t // 2, t % 2
    z, y = g // SIDE, g % SIDE
    def wrap(v):
        return (v + SIDE) % SIDE

    def grp_of(zz, yy):
        return zz * SIDE + yy

    x_next = (g, wrap(x + 1) * 2 + c)
    x_prev = (g, wrap(x - 1) * 2 + c)
    sibling = (g, x * 2 + 1 - c)
    plane = (
        grp_of(wrap(z + 1), y),
        grp_of(wrap(z - 1), y),
        grp_of(z, wrap(y + 1)),
        grp_of(z, wrap(y - 1)),
    )
    P_NEXT, P_PREV, Q_NEXT, Q_PREV = 0, 1, 2, 3

    source = (z + y) % 2 == c
    relay = jnp.logical_not(source)
    x_col = pl.multiple_of(x * COLS, COLS)
    deep = WIDTH // 2

    class Walk:
        def __init__(self, m):
            self.m = m
            self.z_first = c == m
            self.p = jnp.where(self.z_first, z, y)
            self.q = jnp.where(self.z_first, y, z)
            z_ways, y_ways = plane[:2], plane[2:]
            self.ways = [
                (jnp.where(self.z_first, a, b), t)
                for a, b in zip(z_ways + y_ways, y_ways + z_ways)
            ]

        def slot(self, dp, dq):
            pp, qq = wrap(self.p + dp), wrap(self.q + dq)
            zz = jnp.where(self.z_first, pp, qq)
            yy = jnp.where(self.z_first, qq, pp)
            return yy * 2 + zz // 2

        def own(self, h):
            ref = (gate_in, up_in)[self.m]
            return ref.at[pl.ds(h * deep, deep), pl.ds(x_col, COLS)]

        def piece(self, slot, h):
            return wbuf.at[slot, self.m, pl.ds(h * deep, deep)]

        def copy(self, slot, h, way, src=None):
            return pltpu.make_async_remote_copy(
                src_ref=self.piece(slot, h) if src is None else src,
                dst_ref=self.piece(slot, h),
                send_sem=w_send.at[self.m, way, slot * 2 + h],
                recv_sem=w_recv.at[self.m, slot * 2 + h],
                device_id=self.ways[way],
                device_id_type=MESH,
            )

        def wait(self, slot, h):
            self.copy(slot, h, 0).wait_recv()

        def pass_on(self, dp, dq, h, *ways):
            slot = self.slot(dp, dq)
            self.wait(slot, h)
            for way in ways:
                self.copy(slot, h, way).start()

    walks = (Walk(0), Walk(1))
    own_slot = walks[0].slot(0, 0)

    load_own = [
        pltpu.make_async_copy(
            w.own(h), w.piece(own_slot, h), local_sem.at[9 + 2 * w.m + h]
        )
        for h in range(2)
        for w in walks
    ]

    @pl.when(source)
    def _():
        for load in load_own:
            load.start()

    barrier = pltpu.get_barrier_semaphore()
    for there in plane:
        pl.semaphore_signal(
            barrier, inc=1, device_id=(there, t), device_id_type=MESH
        )
    for d in range(1, N_TOK):
        pl.semaphore_signal(
            barrier, inc=1, device_id=(g, (t + d) % N_TOK), device_id_type=MESH
        )
    pl.semaphore_wait(barrier, N_TOK + 3)

    @pl.when(source)
    def _():
        for i in range(4):
            load_own[i].wait()
            for way in range(4):
                walks[i % 2].copy(own_slot, i // 2, way).start()

    def near_first():
        @pl.when(relay)
        def _():
            for w in walks:
                w.pass_on(-1, 0, 0, P_NEXT, Q_NEXT, Q_PREV)
                w.pass_on(1, 0, 0, Q_NEXT, Q_PREV)
            for w in walks:
                w.pass_on(0, -1, 0, Q_NEXT)

    def near_second():
        @pl.when(relay)
        def _():
            for w in walks:
                w.pass_on(1, 0, 1, P_PREV, Q_NEXT, Q_PREV)
                w.pass_on(-1, 0, 1, Q_NEXT, Q_PREV)
            for w in walks:
                w.pass_on(0, 1, 1, Q_PREV)

    def far_half(h):
        @pl.when(source)
        def _():
            for w in walks:
                w.pass_on(2, 0, h, Q_NEXT, Q_PREV)

    def rows_first():
        for w in walks:
            @pl.when(source)
            def _(w=w):
                w.pass_on(-1, -1, 0, Q_NEXT)
                w.pass_on(1, -1, 0, Q_NEXT)

    def rows_far_first():
        for w in walks:
            @pl.when(relay)
            def _(w=w):
                w.pass_on(2, -1, 0, Q_NEXT)

    def rows_second():
        for w in walks:
            @pl.when(source)
            def _(w=w):
                w.pass_on(-1, 1, 1, Q_PREV)
                w.pass_on(1, 1, 1, Q_PREV)

    def rows_far_second():
        for w in walks:
            @pl.when(relay)
            def _(w=w):
                w.pass_on(2, 1, 1, Q_PREV)

    def ring(buf, send, recv, cols=None):
        def copy(slot, n_send, n_recv, there, part=None, src=None):
            ref = buf.at[slot]
            if part is not None:
                ref = ref.at[pl.ds(part * half, half)]
            if cols is not None:
                ref = ref.at[:, pl.ds(*cols)]
            return pltpu.make_async_remote_copy(
                src_ref=ref if src is None else src,
                dst_ref=ref,
                send_sem=send.at[n_send],
                recv_sem=recv.at[n_recv],
                device_id=there,
                device_id_type=MESH,
            )

        prev_s = wrap(x - 1) * 2 + c
        next_s = wrap(x + 1) * 2 + c
        far_s = wrap(x + 2) * 2 + c
        other = 1 - 2 * c

        def begin(src=None):
            copy(t, 0, 0, x_next, src=src).start()
            copy(t, 1, 1, x_prev, src=src).start()
            copy(t, 2, 4, sibling, src=src).start()

        def relay_near():
            copy(prev_s, 0, 0, x_next).wait_recv()
            copy(prev_s, 3, 2, x_next, part=0).start()
            copy(prev_s, 4, 5, sibling).start()
            copy(next_s, 1, 1, x_prev).wait_recv()
            copy(next_s, 5, 3, x_prev, part=1).start()
            copy(next_s, 6, 6, sibling).start()

        def relay_far():
            copy(far_s, 3, 2, x_next, part=0).wait_recv()
            copy(far_s, 7, 7, sibling, part=0).start()
            copy(far_s, 5, 3, x_prev, part=1).wait_recv()
            copy(far_s, 8, 8, sibling, part=1).start()

        def sibling_own():
            copy(t + other, 2, 4, sibling).wait_recv()

        def sibling_near():
            copy(prev_s + other, 4, 5, sibling).wait_recv()
            copy(next_s + other, 6, 6, sibling).wait_recv()

        def sibling_far():
            copy(far_s + other, 7, 7, sibling, part=0).wait_recv()
            copy(far_s + other, 8, 8, sibling, part=1).wait_recv()

        def drain():
            copy(t, 0, 0, x_next).wait_send()
            copy(t, 1, 1, x_prev).wait_send()
            copy(t, 2, 4, sibling).wait_send()
            copy(prev_s, 3, 2, x_next, part=0).wait_send()
            copy(prev_s, 4, 5, sibling).wait_send()
            copy(next_s, 5, 3, x_prev, part=1).wait_send()
            copy(next_s, 6, 6, sibling).wait_send()
            copy(far_s, 7, 7, sibling, part=0).wait_send()
            copy(far_s, 8, 8, sibling, part=1).wait_send()

        return (
            begin,
            relay_near,
            relay_far,
            sibling_own,
            sibling_near,
            sibling_far,
            drain,
        )

    kv_ring = ring(kvbuf, kv_send, kv_recv)
    kv_ring[0](kv_in)

    def seg_copy(d):
        return pltpu.make_async_remote_copy(
            src_ref=seg_in,
            dst_ref=segbuf.at[t],
            send_sem=seg_send,
            recv_sem=seg_recv,
            device_id=(g, (t + d) % N_TOK),
            device_id_type=MESH,
        )

    for d in range(1, N_TOK):
        seg_copy(d).start()

    load_kv = pltpu.make_async_copy(kv_in, kvbuf.at[t], local_sem.at[0])
    load_q = pltpu.make_async_copy(q_in, qbuf, local_sem.at[1])
    load_res = pltpu.make_async_copy(res_in, resbuf, local_sem.at[2])
    load_cache = pltpu.make_async_copy(cache_in, cachebuf, local_sem.at[3])
    load_seg = pltpu.make_async_copy(seg_in, segbuf.at[t], local_sem.at[4])
    load_kv.start()
    load_q.start()
    load_seg.start()
    load_res.start()
    load_cache.start()

    load_seg.wait()
    pltpu.make_async_copy(segbuf.at[pl.ds(0, N_TOK - 1)], segbuf.at[pl.ds(0, N_TOK - 1)], seg_recv).wait()
    own_seg = jnp.broadcast_to(seg_in[...], (rows, rows)).T
    row_id = lax.broadcasted_iota(jnp.int32, (rows, rows), 0) + t * rows
    col_id = lax.broadcasted_iota(jnp.int32, (rows, rows), 1)
    for i in range(N_TOK):
        live = (own_seg == segbuf[i]) & (col_id + i * rows <= row_id)
        biasbuf[:, i * rows : (i + 1) * rows] = jnp.where(live, 0.0, MASKED)

    kv_ring[1]()

    near_first()
    kv_ring[2]()
    load_kv.wait()
    load_q.wait()
    load_res.wait()
    kv_ring[3]()
    kv_ring[4]()
    kv_ring[5]()

    scale = 1.0 / math.sqrt(HEAD)

    def attend(h, squares):
        base = pl.multiple_of(h * (GROUP * HEAD), HEAD)
        queries = jnp.concatenate(
            [qbuf[:, pl.ds(base + j * HEAD, HEAD)] for j in range(GROUP)], axis=0
        )
        k_col = pl.multiple_of(h * HEAD, HEAD)
        k = kvbuf[:, :, pl.ds(k_col, HEAD)].reshape(keys, HEAD)
        v = kvbuf[:, :, pl.ds(k_col + KV_HEADS * HEAD, HEAD)].reshape(keys, HEAD)
        scores = lax.dot_general(
            queries, k, (((1,), (1,)), ((), ())), preferred_element_type=jnp.float32
        )
        scores = scores.reshape(GROUP, rows, keys) + biasbuf[...][None]
        top = jnp.max(scores, axis=-1, keepdims=True)
        weights = jnp.exp((scores - top) * scale)
        total = jnp.sum(weights, axis=-1, keepdims=True)
        weights = weights.astype(jnp.bfloat16).reshape(GROUP * rows, keys)
        out = jnp.dot(weights, v, preferred_element_type=jnp.float32)
        out = (out.reshape(GROUP, rows, HEAD) / total).astype(jnp.bfloat16)
        for j in range(GROUP):
            cols = pl.ds(base + j * HEAD, HEAD)
            a = resbuf[:, cols].astype(jnp.float32) + out[j].astype(jnp.float32)
            a = a.astype(jnp.bfloat16)
            att_out[:, cols] = a
            a = a.astype(jnp.float32)
            normbuf[t, :, cols] = (a * gain_in[:, cols]).astype(jnp.bfloat16)
            squares = squares + a * a
        return squares

    width = 2 * GROUP * HEAD
    rings = [
        ring(normbuf, nrm_send.at[i], nrm_recv.at[i], (i * width, width))
        for i in range(KV_HEADS // 2)
    ]
    squares = jnp.zeros((rows, HEAD), jnp.float32)
    squares = lax.fori_loop(0, 2, attend, squares)
    rings[0][0]()
    far_half(0)
    squares = lax.fori_loop(2, 4, attend, squares)
    rings[1][0]()
    near_second()
    squares = lax.fori_loop(4, 6, attend, squares)
    rings[2][0]()
    rings[0][1]()
    squares = lax.fori_loop(6, 8, attend, squares)
    rings[3][0]()
    mean = jnp.sum(squares, axis=-1, keepdims=True) * (1.0 / WIDTH)
    inverse = jnp.broadcast_to(lax.rsqrt(mean + 1e-6), (rows, rows))
    scalebuf[t] = inverse
    statbuf[t] = inverse.T[:1]

    def stat_copy(d):
        return pltpu.make_async_remote_copy(
            src_ref=statbuf.at[t],
            dst_ref=statbuf.at[t],
            send_sem=stat_send,
            recv_sem=stat_recv,
            device_id=(g, (t + d) % N_TOK),
            device_id_type=MESH,
        )

    for d in range(1, N_TOK):
        stat_copy(d).start()
    far_half(1)
    rings[0][2]()
    rows_first()
    rings[1][1]()

    load_cache.wait()
    table = jnp.broadcast_to(table_in[...], (8, table_in.shape[1]))
    page_id = lax.broadcasted_iota(jnp.int32, (table_in.shape[1], keys), 0)
    key_id = lax.broadcasted_iota(jnp.int32, (table_in.shape[1], keys), 1)
    spread = (page_id == key_id // PAGE).astype(jnp.float32).astype(jnp.bfloat16)
    slot_of = jnp.dot(
        table.astype(jnp.float32).astype(jnp.bfloat16),
        spread,
        preferred_element_type=jnp.float32,
    )
    key_row = lax.broadcasted_iota(jnp.int32, (8, keys), 1)
    key_row = (key_row % PAGE).astype(jnp.float32)
    shift = (t * slots_here).astype(jnp.float32)
    goal = ((slot_of - shift) * PAGE + key_row)[:1]
    here = lax.broadcasted_iota(jnp.int32, (slots_here * PAGE, keys), 0)
    picked = (here.astype(jnp.float32) == goal).astype(jnp.float32)
    covered = jnp.sum(picked, axis=-1, keepdims=True) > 0.5
    picked = picked.astype(jnp.bfloat16)
    chunk = 512

    def place(i, carry):
        cols = pl.ds(pl.multiple_of(i * chunk, chunk), chunk)
        rows_kv = kvbuf[:, :, cols].reshape(keys, chunk)
        new = jnp.dot(picked, rows_kv, preferred_element_type=jnp.float32)
        old = cachebuf[:, :, cols].reshape(slots_here * PAGE, chunk)
        both = jnp.where(covered, new, old.astype(jnp.float32)).astype(jnp.bfloat16)
        cache_out[:, :, cols] = both.reshape(slots_here, PAGE, chunk)
        return carry

    lax.fori_loop(0, kv_in.shape[1] // chunk, place, 0)

    rows_far_first()
    rings[1][2]()
    rings[2][1]()
    rows_second()
    rings[2][2]()
    rings[3][1]()
    some = statbuf.at[pl.ds(0, N_TOK - 1)]
    pltpu.make_async_copy(some, some, stat_recv).wait()

    def spread_scale(d, carry):
        there = (t + d) % N_TOK
        scalebuf[there] = jnp.broadcast_to(statbuf[there], (rows, rows)).T
        return carry

    lax.fori_loop(1, N_TOK, spread_scale, 0)
    rows_far_second()
    rings[3][2]()
    for part in rings:
        part[3]()
        part[4]()
        part[5]()

    parts = 1
    per = N_TOK // parts

    def choose(i, values):
        out = jnp.int32(values[-1])
        for k in range(len(values) - 1):
            out = jnp.where(i == k, values[k], out)
        return out

    def project(i, carry):
        dz = jnp.where(
            source,
            choose(i, (0, 2, 0, 1, 1, 3, 3, 2)),
            choose(i, (1, 3, 0, 0, 3, 2, 1, 2)),
        )
        dy = jnp.where(
            source,
            choose(i, (0, 0, 2, 1, 3, 1, 3, 2)),
            choose(i, (0, 0, 1, 3, 2, 3, 2, 1)),
        )
        zz, yy = wrap(z + dz), wrap(y + dy)
        slot = yy * 2 + zz // 2
        for w in walks:
            dq = jnp.where(w.z_first, dy, dz)

            @pl.when((dq == 1) | (dq == 2))
            def _(w=w):
                w.wait(slot, 0)

            @pl.when((dq == 3) | (dq == 2))
            def _(w=w):
                w.wait(slot, 1)

        column = pl.multiple_of(grp_of(zz, yy) * units + x_col, COLS)

        def tile(k, carry):
            some = pl.ds(k * per, per)
            tokens = normbuf[some].reshape(per * rows, WIDTH)
            both = jnp.concatenate([wbuf[slot, 0], wbuf[slot, 1]], axis=1)
            sums = jnp.dot(tokens, both, preferred_element_type=jnp.float32)
            scale = scalebuf[some].reshape(per * rows, COLS)
            gate, up = sums[:, :COLS] * scale, sums[:, COLS:] * scale
            value = gate / (1.0 + jnp.exp(-gate)) * up
            hidbuf[slot, some] = value.astype(jnp.bfloat16).reshape(per, rows, COLS)
            return carry

        lax.fori_loop(0, parts, tile, 0)
        pltpu.make_async_copy(
            hidbuf.at[slot, t], hid_out.at[:, pl.ds(column, COLS)], hid_recv
        ).start()

        def send(d, carry):
            there = (t + d) % N_TOK
            pltpu.make_async_remote_copy(
                src_ref=hidbuf.at[slot, there],
                dst_ref=hid_out.at[:, pl.ds(column, COLS)],
                send_sem=hid_send,
                recv_sem=hid_recv,
                device_id=(g, there),
                device_id_type=MESH,
            ).start()
            return carry

        lax.fori_loop(1, N_TOK, send, 0)
        return carry

    lax.fori_loop(0, 8, project, 0)

    pltpu.make_async_copy(
        segbuf.at[pl.ds(0, N_TOK - 1)], segbuf.at[pl.ds(0, N_TOK - 1)], seg_send
    ).wait()
    kv_ring[6]()
    pltpu.make_async_copy(some, some, stat_send).wait()
    for part in rings:
        part[6]()

    @pl.when(source)
    def _():
        for w in walks:
            for h in range(2):
                for way in range(4):
                    w.copy(own_slot, h, way).wait_send()
                w.copy(w.slot(2, 0), h, Q_NEXT).wait_send()
                w.copy(w.slot(2, 0), h, Q_PREV).wait_send()
            for dp in (-1, 1):
                w.copy(w.slot(dp, -1), 0, Q_NEXT).wait_send()
                w.copy(w.slot(dp, 1), 1, Q_PREV).wait_send()

    @pl.when(relay)
    def _():
        for w in walks:
            w.copy(w.slot(-1, 0), 0, P_NEXT).wait_send()
            w.copy(w.slot(1, 0), 1, P_PREV).wait_send()
            for h in range(2):
                for dp in (-1, 1):
                    w.copy(w.slot(dp, 0), h, Q_NEXT).wait_send()
                    w.copy(w.slot(dp, 0), h, Q_PREV).wait_send()
            for dp in (0, 2):
                w.copy(w.slot(dp, -1), 0, Q_NEXT).wait_send()
                w.copy(w.slot(dp, 1), 1, Q_PREV).wait_send()

    whole = hidbuf.at[:, pl.ds(0, N_TOK - 1)]
    pltpu.make_async_copy(whole, whole, hid_send).wait()
    pltpu.make_async_copy(hidbuf, hidbuf, hid_recv).wait()


def on_device(
    queries,
    rotated_keys_values,
    prompt_window_index,
    residual,
    ffn_gain,
    gate_weight,
    up_weight,
    paged_cache,
    page_table,
):
    rows = queries.shape[0]
    kv_width = rotated_keys_values.shape[1]
    hidden_width = gate_weight.shape[1] * SIDE * SIDE
    any_space = pl.BlockSpec(memory_space=pl.ANY)
    vmem = pl.BlockSpec(memory_space=pltpu.VMEM)
    bf16 = jnp.bfloat16
    dma = pltpu.SemaphoreType.DMA
    outs = pl.pallas_call(
        kernel,
        out_shape=(
            pltpu.VMEM(residual.shape, bf16),
            pltpu.VMEM((rows, hidden_width), bf16),
            pltpu.VMEM(paged_cache.shape, bf16),
        ),
        in_specs=[
            any_space,
            any_space,
            vmem,
            any_space,
            vmem,
            any_space,
            any_space,
            any_space,
            vmem,
        ],
        out_specs=(vmem, vmem, vmem),
        scratch_shapes=[
            pltpu.VMEM(queries.shape, bf16),
            pltpu.VMEM((N_TOK, rows, kv_width), bf16),
            pltpu.VMEM((N_TOK, 1, rows), jnp.int32),
            pltpu.VMEM(residual.shape, bf16),
            pltpu.VMEM(paged_cache.shape, bf16),
            pltpu.VMEM((rows, N_TOK * rows), jnp.float32),
            pltpu.VMEM((N_TOK, 1, rows), jnp.float32),
            pltpu.VMEM((N_TOK, rows, COLS), jnp.float32),
            pltpu.VMEM((N_TOK, rows, WIDTH), bf16),
            pltpu.VMEM((8, 2, WIDTH, COLS), bf16),
            pltpu.VMEM((8, N_TOK, rows, COLS), bf16),
            dma((9,)),
            dma((9,)),
            dma((KV_HEADS // 2, 9)),
            dma((KV_HEADS // 2, 9)),
            dma((2, 4, 16)),
            dma((2, 16)),
            dma(()),
            dma(()),
            dma(()),
            dma(()),
            dma(()),
            dma(()),
            dma((13,)),
        ],
        compiler_params=pltpu.CompilerParams(
            collective_id=0,
            has_side_effects=True,
            vmem_limit_bytes=50 * 1024 * 1024,
        ),
        name="layer",
    )(
        queries,
        rotated_keys_values,
        prompt_window_index,
        residual,
        ffn_gain.reshape(1, -1),
        gate_weight,
        up_weight,
        paged_cache,
        page_table,
    )
    return tuple(outs)


def solution(mesh):
    in_specs = (
        P(("grp", "tok"), None),
        P(("grp", "tok"), None),
        P("grp", "tok"),
        P(("grp", "tok"), None),
        P(),
        P(None, "grp"),
        P(None, "grp"),
        P(("grp", "tok"), None, None),
        P("grp", None),
    )
    out_specs = (P(("grp", "tok"), None), P(("grp", "tok"), None), P(("grp", "tok"), None, None))
    return jax.shard_map(
        on_device, mesh=mesh, in_specs=in_specs, out_specs=out_specs, check_vma=False
    )
```
